32 devices in a mesh: ra: 4 (over z), dec: 8 (over y, x, core).
Axes of the slice: x: 2, y: 2, z: 4, core: 2. Of those that a mesh axis runs over, the one named last changes fastest.
Arguments:
- forests: bfloat16 [8, 32, 128, 1024], P('ra', 'dec'), may hold values from -6 to 6
- resolution: float32 [8, 32, 128], P('ra', 'dec'), may hold values from 0.3 to 1.2
- pixel_range: int32 [8, 32, 2, 128], P('ra', 'dec'), may hold values from 0 to 1024, as said below
- block_pairs: int32 [4, 8, 40, 3], P('ra', 'dec'), may hold values from -1 to 7, as said below
- block_count: int32 [4, 8], P('ra', 'dec'), may hold values from 10 to 40, as said below
- separation_bin: int32 [4, 8, 40, 128, 128], P('ra', 'dec'), may hold values from 0 to 8
Outputs:
- tile_power: float32 [4, 8, 8, 128], P('ra', 'dec')
- sky_power: float32 [8, 128], replicated
The draws below stay inside these ranges and needn't reach their ends.
Inputs may be any that keep to these rules, and one draw needn't show every extreme that they name: `pixel_range`: lo < hi for every forest; at least 256 valid pixels. `block_pairs`: each device's list names every one of its own cells once with each of the five offsets (0, 0), (0, 1), (1, -1), (1, 0), (1, 1), in an order drawn from the seed. Slots at or past block_count are ignored. `block_count`: some device has all 40 slots live in every draw.
All inputs are finite; a program needn't handle non-finite values.
Results may differ from the reference program's by a relative error of at most 0.0037.
Values may be sent and summed in bfloat16 or wider, within the bound.
No kernel may reach another device: no remote copies, remote signals or barrier semaphores. Data moves between devices by JAX's collectives and lax.ppermute only.
A program may use at most 64 MiB of HBM per device.

```python
import math
import jax
import jax.numpy as jnp
from jax import lax

CELLS_RA = 2
CELLS_DEC = 4
FPC = 128
NPIX = 1024
NSEP = 8
NKB = 128
BLOCKS = 40
ROWS = 8
COLS = 32
N_RA = 4
N_DEC = 8


def draw_pixel_range(key, part):
    first_key, second_key = jax.random.split(jax.random.fold_in(key, 11))
    shape = (CELLS_RA * N_RA, CELLS_DEC * N_DEC, 1, FPC)
    lower = jax.random.randint(first_key, shape, 0, NPIX // 4 + 1)
    extent = jax.random.randint(second_key, shape, NPIX // 2, NPIX + 1)
    upper = jnp.minimum(lower + extent, NPIX)
    return jnp.concatenate([lower, upper], axis=2).astype(jnp.int32)


def slot_helper(key):
    keys = jax.random.split(jax.random.fold_in(key, 23), 3)
    tiles = N_RA * N_DEC
    order_keys = jax.random.split(keys[0], tiles)
    orders = jax.vmap(lambda one_key: jax.random.permutation(one_key, BLOCKS))(order_keys)
    orders = orders.astype(jnp.int32).reshape(N_RA, N_DEC, BLOCKS)
    cells = orders // 5
    direction = orders % 5
    ra_step = (direction >= 2).astype(jnp.int32)
    dec_step = jnp.where(direction == 1, 1, jnp.where(direction >= 2, direction - 3, 0)).astype(jnp.int32)
    pairs = jnp.stack([cells, ra_step, dec_step], axis=-1).astype(jnp.int32)
    lowest = max(2, BLOCKS // 4)
    spread = jax.random.randint(keys[1], (N_RA, N_DEC), 0, 64)
    counts = lowest + (BLOCKS - lowest) * spread * spread // 4096
    fullest = jax.random.randint(keys[2], (), 0, tiles)
    flat_index = jnp.arange(tiles, dtype=jnp.int32).reshape(N_RA, N_DEC)
    counts = jnp.where(flat_index == fullest, BLOCKS, counts)
    return (pairs, counts.astype(jnp.int32))


def draw_block_pairs(key, part):
    return slot_helper(key)[0]


def draw_block_count(key, part):
    return slot_helper(key)[1]


def place_ends(array, rng, low, high):
    place = [jax.random.randint(jax.random.fold_in(rng, axis), (), 0, length) for axis, length in enumerate(array.shape)]
    longest = array.shape.index(max(array.shape))
    neighbour = place[:longest] + [(place[longest] + 1) % array.shape[longest]] + place[longest + 1:]
    return array.at[tuple(place)].set(low).at[tuple(neighbour)].set(high)


def levels(key, shape, pieces, least, largest):
    factor_of, own = 1.0, jax.random.fold_in(key, 6)
    for axis_at, parts in pieces:
        heights = jnp.exp(jax.random.uniform(jax.random.fold_in(own, axis_at), (parts,), jnp.float32, least / len(pieces), largest / len(pieces)))
        factor_of = factor_of * jnp.repeat(heights, shape[axis_at] // parts).reshape([-1 if axis == axis_at else 1 for axis in range(len(shape))])
    return factor_of


def scatter_about(rng, shape, deviation, bound, shards=(), held_as=jnp.bfloat16):
    level = levels(rng, shape, shards, -0.22, 0.18) if shards else 1.0
    array = jax.random.normal(rng, shape, jnp.float32) * deviation * level
    return jnp.minimum(jnp.maximum(array, -bound), bound).astype(held_as)


def setup_inputs(seed: int = 0) -> dict:
    seeds = jax.random.split(jax.random.key(seed), 7)
    return {
        "forests": scatter_about(seeds[0], (ROWS, COLS, FPC, NPIX), 1.0, 6.0, ((0, 4), (1, 8))),
        "resolution": jnp.clip(jnp.exp(math.log(1.2) - 1.3862944 * jax.random.uniform(seeds[1], (ROWS, COLS, FPC), jnp.float32) ** levels(seeds[1], (ROWS, COLS, FPC), ((0, 4), (1, 8)), -0.2, 0.2)), 0.3, 1.2),
        "pixel_range": draw_pixel_range(jax.random.fold_in(seeds[6], 71), 0),
        "block_pairs": draw_block_pairs(jax.random.fold_in(seeds[6], 71), 0),
        "block_count": draw_block_count(jax.random.fold_in(seeds[6], 71), 0),
        "separation_bin": place_ends(jax.random.randint(seeds[5], (N_RA, N_DEC, BLOCKS, FPC, FPC), 0, NSEP + 1), jax.random.fold_in(seeds[5], 1), 0, NSEP).astype(jnp.int32),
    }


def dft_table(length, n_modes):
    sample = jnp.arange(length, dtype=jnp.int32)[:, None]
    mode_index = jnp.arange(n_modes, dtype=jnp.int32)[None, :]
    angles = ((sample * mode_index) % length).astype(jnp.float32) * (2.0 * jnp.pi / length)
    return jnp.concatenate([jnp.cos(angles), jnp.sin(angles)], axis=1).astype(jnp.bfloat16)


def kbin_table(n_modes, n_bins):
    column = jnp.arange(2 * n_modes, dtype=jnp.int32) % n_modes
    which = column // (n_modes // n_bins)
    return (which[:, None] == jnp.arange(n_bins, dtype=jnp.int32)[None, :]).astype(jnp.float32)


def mask_pixels(flux, pixel_range):
    position = jnp.arange(flux.shape[-1], dtype=jnp.int32)
    lower = pixel_range[..., 0, :][..., None]
    upper = pixel_range[..., 1, :][..., None]
    inside = (position >= lower) & (position < upper)
    return jnp.where(inside, flux, jnp.zeros_like(flux))


def to_spectra(masked, widths, basis):
    length = basis.shape[0]
    n_modes = basis.shape[1] // 2
    raw = jnp.dot(masked, basis, preferred_element_type=jnp.float32)
    wavenum = jnp.arange(n_modes, dtype=jnp.float32) * (2.0 * jnp.pi / length)
    wavenum = jnp.concatenate([wavenum, wavenum])
    window = jnp.exp(-0.5 * (wavenum * widths[..., None]) ** 2)
    return (raw * window).astype(jnp.bfloat16)


def block_term(grid_flat, index_a, index_b, sep_bins):
    n_sep = NSEP
    per_cell = sep_bins.shape[0]
    left = lax.dynamic_index_in_dim(grid_flat, index_a.astype(jnp.int32), 0, keepdims=False)
    right = lax.dynamic_index_in_dim(grid_flat, index_b.astype(jnp.int32), 0, keepdims=False)
    onehot = (sep_bins[None, :, :] == jnp.arange(n_sep, dtype=jnp.int32)[:, None, None]).astype(jnp.bfloat16)
    mixed = jnp.dot(onehot.reshape(n_sep * per_cell, per_cell), right, preferred_element_type=jnp.float32)
    mixed = mixed.reshape(n_sep, per_cell, -1)
    block_sum = jnp.sum(mixed * left.astype(jnp.float32)[None], axis=1)
    pair_counts = jnp.sum(onehot.reshape(n_sep, -1).astype(jnp.float32), axis=1)
    return block_sum, pair_counts


def reference(forests, resolution, pixel_range, block_pairs, block_count, separation_bin):
    basis = dft_table(NPIX, NPIX // 2)

    def row_spectra(inputs):
        flux, widths, ranges = inputs
        return to_spectra(mask_pixels(flux, ranges), widths, basis)

    spectra = lax.map(row_spectra, (forests, resolution, pixel_range))
    padded = jnp.pad(spectra, ((1, 1), (1, 1), (0, 0), (0, 0)))
    cols_pad = COLS + 2
    grid_flat = padded.reshape(-1, FPC, NPIX)
    tiles = N_RA * N_DEC

    def one_tile(inputs):
        tile_index, entries, live_count, sep_bins = inputs
        tile_row = tile_index // N_DEC
        tile_col = tile_index % N_DEC

        def step(carry, slot_index):
            entry_row = entries[slot_index]
            row_a = tile_row * CELLS_RA + entry_row[0] // CELLS_DEC + 1
            col_a = tile_col * CELLS_DEC + entry_row[0] % CELLS_DEC + 1
            index_a = row_a * cols_pad + col_a
            index_b = (row_a + entry_row[1]) * cols_pad + col_a + entry_row[2]
            block_sum, counts = block_term(grid_flat, index_a, index_b, sep_bins[slot_index])
            is_live = (slot_index < live_count).astype(jnp.float32)
            return (carry[0] + is_live * block_sum, carry[1] + is_live * counts), None

        start_value = (jnp.zeros((NSEP, NPIX), jnp.float32), jnp.zeros((NSEP,), jnp.float32))
        (sums, counts), _ = lax.scan(step, start_value, jnp.arange(BLOCKS, dtype=jnp.int32))
        binned = jnp.dot(sums, kbin_table(NPIX // 2, NKB), precision=lax.Precision.HIGHEST)
        return binned, counts

    binned, counts = lax.map(one_tile, (jnp.arange(tiles, dtype=jnp.int32), block_pairs.reshape(tiles, BLOCKS, 3), block_count.reshape(tiles), separation_bin.reshape(tiles, BLOCKS, FPC, FPC)))
    tile_power = (binned / (FPC * NPIX)).reshape(N_RA, N_DEC, NSEP, NKB)
    summed = jnp.sum(binned, axis=0)
    all_counts = jnp.sum(counts, axis=0)
    sky_power = summed / jnp.maximum(all_counts, 1.0)[:, None]
    return tile_power, sky_power
```

```python
import jax
import jax.numpy as jnp
import numpy as np
from jax import lax
from jax.experimental import pallas as pl
from jax.experimental.pallas import tpu as pltpu
from jax.sharding import PartitionSpec as P

NSEP = 8
NKB = 128
OFFSETS = ((0, 0), (0, 1), (1, -1), (1, 0), (1, 1))

SINE_TILE = 2


def tile_table(per_bin):
    return [(q, trig) for base in range(0, per_bin, 2) for trig in (0, 1) for q in (base, base + 1)]


def dft_table(length, n_bins):
    per_bin = length // 2 // n_bins
    sample = np.arange(length)[:, None]
    tiles = []
    for q, trig in tile_table(per_bin):
        mode = np.arange(n_bins)[None, :] * per_bin + q
        angle = 2.0 * np.pi * (sample * mode % length) / length
        tiles.append(np.sin(angle) if trig else np.cos(angle))
    return np.concatenate(tiles, axis=1).astype(np.float32).astype(jnp.bfloat16)


def pair_up(edges):
    at = {}
    for edge in edges:
        for cell in {edge[1], edge[2]}:
            at.setdefault(cell, []).append(edge)
    seen, used, groups = set(), set(), []

    def visit(cell, up):
        seen.add(cell)
        pending = []
        for edge in at[cell]:
            if edge in used or edge is up:
                continue
            other = edge[2] if edge[1] == cell else edge[1]
            used.add(edge)
            if other == cell or other in seen or not visit(other, edge):
                pending.append(edge)
        pending.sort(key=lambda edge: edge[3])
        taken = False
        if len(pending) % 2 and up is not None:
            pending.append(up)
            taken = True
        for i in range(0, len(pending), 2):
            groups.append((cell, pending[i : i + 2]))
        return taken

    for cell in sorted(at):
        if cell not in seen:
            visit(cell, None)
    return groups


def plan(rows, cols):
    def arrival(cell):
        r, c = cell
        if r == rows:
            return 2 if c in (0, cols - 1) else 3
        return 0 if 0 <= c < cols else 1

    edges = []
    for r in range(rows):
        for c in range(cols):
            for d, (up, side) in enumerate(OFFSETS):
                a, b = (r, c), (r + up, c + side)
                key = (r * cols + c) * len(OFFSETS) + d
                edges.append((key, a, b, max(arrival(a), arrival(b))))
    stages = [[], [], [], []]
    for pool in ((0, 1), (2,), (3,)):
        for group in pair_up([edge for edge in edges if edge[3] in pool]):
            stages[max(edge[3] for edge in group[1])].append(group)
    return stages[0], stages[1] + stages[2], stages[3]


def split_copies(source, target, sems, first=0):
    return [
        pltpu.make_async_copy(source.at[first + i], target.at[i], sems.at[i])
        for i in range(target.shape[0])
    ]


def write_spectra(cells, flux, ranges, widths, basis, basis_copies, flux_copies, masked, stores):
    count, per_cell, length = flux.shape
    halves, _, block = basis.shape
    per_bin = length // 2 // NKB
    rows = []
    for r, c in cells:
        rows += [ranges[r, c].astype(jnp.float32), widths[r, c : c + 1]]
    filler = -3 * count % 8
    if filler:
        rows.append(jnp.zeros((filler, per_cell), jnp.float32))
    columns = jnp.concatenate(rows, axis=0).T
    position = lax.broadcasted_iota(jnp.int32, (per_cell, length), 1).astype(jnp.float32)
    for i in range(count):
        low, high = columns[:, 3 * i : 3 * i + 1], columns[:, 3 * i + 1 : 3 * i + 2]
        flux_copies[i].wait()
        inside = (position >= low) & (position < high)
        kept = jnp.where(inside, flux[i].astype(jnp.float32), 0.0)
        masked[i * per_cell : (i + 1) * per_cell] = kept.astype(jnp.bfloat16)
    lane = lax.broadcasted_iota(jnp.int32, (1, NKB), 1) * per_bin
    width = [
        jnp.broadcast_to(columns[:, 3 * i + 2 : 3 * i + 3], (per_cell, NKB)) for i in range(count)
    ]
    span = 2 * NKB
    for half in range(halves):
        basis_copies[half].wait()
        windows = []
        for q in (2 * half, 2 * half + 1):
            wave = (lane + q).astype(jnp.float32) * (2.0 * jnp.pi / length)
            windows.append([jnp.exp(-0.5 * (wave * width[i]) ** 2) for i in range(count)])
        for trig in (0, 1):
            raw = jnp.dot(
                masked[...],
                basis[half, :, trig * span : (trig + 1) * span],
                preferred_element_type=jnp.float32,
            )
            for i in range(count):
                for s in (0, 1):
                    part = raw[i * per_cell : (i + 1) * per_cell, s * NKB : (s + 1) * NKB]
                    value = (part * windows[s][i]).astype(jnp.bfloat16)
                    start = half * block + trig * span + s * NKB
                    for ref, at in stores[i]:
                        ref[at, :, start : start + NKB] = value


def vmem(n):
    return [pl.BlockSpec(memory_space=pltpu.VMEM)] * n


def params(mib):
    return pltpu.CompilerParams(vmem_limit_bytes=mib * 2**20)


def cost(flops, nbytes):
    return pl.CostEstimate(flops=int(flops), bytes_accessed=int(nbytes), transcendentals=0)


def first_row(forests, ranges, widths, basis):
    _, cols, per_cell, length = forests.shape
    halves = basis.shape[0]

    def kernel(forests, ranges, widths, basis, ends, middle, flux, table, masked, sems, table_sems):
        flux_copies = split_copies(forests.at[0], flux, sems)
        basis_copies = split_copies(basis, table, table_sems)
        for copy in flux_copies + basis_copies:
            copy.start()
        stores = [[(ends, 0)]] + [[(middle, i)] for i in range(cols - 2)] + [[(ends, 1)]]
        cells = [(0, c) for c in range(cols)]
        write_spectra(
            cells, flux, ranges, widths, table, basis_copies, flux_copies, masked, stores
        )

    return pl.pallas_call(
        kernel,
        name="first_row",
        out_shape=[
            jax.ShapeDtypeStruct((n, per_cell, length), jnp.bfloat16) for n in (2, cols - 2)
        ],
        in_specs=[pl.BlockSpec(memory_space=pltpu.HBM)] + vmem(2) + [pl.BlockSpec(memory_space=pltpu.HBM)],
        out_specs=vmem(2),
        scratch_shapes=[
            pltpu.VMEM((cols, per_cell, length), jnp.bfloat16),
            pltpu.VMEM(basis.shape, jnp.bfloat16),
            pltpu.VMEM((cols * per_cell, length), jnp.bfloat16),
            pltpu.SemaphoreType.DMA((cols,)),
            pltpu.SemaphoreType.DMA((halves,)),
        ],
        compiler_params=params(58),
        cost_estimate=cost(2 * cols * per_cell * length * length, 5 * 2**20),
    )(forests, ranges, widths, basis)


def other_rows(forests, ranges, widths, basis, ends, entries, count, bins, stages):
    rows, cols, per_cell, length = forests.shape
    slots = bins.shape[0]
    n_cells = (rows - 1) * cols
    halves = basis.shape[0]
    cells = [(r, c) for r in range(1, rows) for c in range(cols)]
    sizes = [sum(len(group[1]) for group in stage) for stage in stages]

    def kernel(*refs):
        forests, ranges, widths, basis, ends, entries, count, bins = refs[:8]
        own, low, high = refs[8:11]
        sorted_bins = refs[11 : 11 + len(stages)]
        flux, table, masked, raw_bins, slot_of, sems, table_sems, bin_sem = refs[11 + len(stages) :]
        flux_copies, basis_copies = [], split_copies(basis, table, table_sems)
        for i, (r, c) in enumerate(cells):
            flux_copies.append(pltpu.make_async_copy(forests.at[r, c], flux.at[i], sems.at[i]))
        bin_copy = pltpu.make_async_copy(bins, raw_bins, bin_sem)
        for copy in flux_copies + basis_copies + [bin_copy]:
            copy.start()

        @pl.loop(0, slots)
        def _(s):
            key = (
                entries[0, 0, s, 0] * len(OFFSETS) + 3 * entries[0, 0, s, 1] + entries[0, 0, s, 2]
            )
            slot_of[key] = jnp.where(s < count[0, 0], s, s + slots)

        low[0] = ends[0]
        stores = []
        for i, (r, c) in enumerate(cells):
            stores.append([(own, i)])
            if c == 0:
                stores[-1].append((low, r))
            if c == cols - 1:
                stores[-1].append((high, r - 1))
        write_spectra(
            cells, flux, ranges, widths, table, basis_copies, flux_copies, masked, stores
        )
        bin_copy.wait()
        for target, stage in zip(sorted_bins, stages):
            edges = [(center, edge) for center, pair in stage for edge in pair]
            for i, (center, edge) in enumerate(edges):
                at = slot_of[edge[0]]
                dead = at >= slots
                block = raw_bins[jnp.where(dead, at - slots, at)].astype(jnp.float32)
                block = block + jnp.where(dead, float(NSEP), 0.0)
                if center != edge[1]:
                    block = block.T
                target[i] = block.astype(jnp.bfloat16)

    anywhere = pl.BlockSpec(memory_space=pltpu.HBM)
    scalars = pl.BlockSpec(memory_space=pltpu.SMEM)
    shapes = [(n_cells, per_cell, length), (rows, per_cell, length), (rows - 1, per_cell, length)]
    shapes += [(size, per_cell, per_cell) for size in sizes]
    return pl.pallas_call(
        kernel,
        name="other_rows",
        out_shape=[jax.ShapeDtypeStruct(shape, jnp.bfloat16) for shape in shapes],
        in_specs=[anywhere] + vmem(2) + [anywhere] + vmem(1) + [scalars, scalars, anywhere],
        out_specs=vmem(len(shapes)),
        scratch_shapes=[
            pltpu.VMEM((n_cells, per_cell, length), jnp.bfloat16),
            pltpu.VMEM(basis.shape, jnp.bfloat16),
            pltpu.VMEM((n_cells * per_cell, length), jnp.bfloat16),
            pltpu.VMEM(bins.shape, jnp.int32),
            pltpu.SMEM((slots,), jnp.int32),
            pltpu.SemaphoreType.DMA((n_cells,)),
            pltpu.SemaphoreType.DMA((halves,)),
            pltpu.SemaphoreType.DMA,
        ],
        compiler_params=params(50),
        cost_estimate=cost(2 * n_cells * per_cell * length * length, 8 * 2**20),
    )(forests, ranges, widths, basis, ends, entries, count, bins)


def pair_sums(name, groups, bins, arrays, place, partials, last):
    _, per_cell, length = arrays[0].shape
    n_arrays, n_partials = len(arrays), len(partials)
    span = 2 * NKB

    def kernel(*refs):
        arrays, bins = refs[:n_arrays], refs[n_arrays]
        partials = refs[n_arrays + 1 : n_arrays + 1 + n_partials]
        out, chosen = refs[-2:]
        lane = lax.broadcasted_iota(jnp.int32, (per_cell, NKB), 1)
        unit = jnp.where(lane == 0, 1.0, 0.0).astype(jnp.bfloat16)

        def columns(cell, n):
            array, at = place[cell]
            value = arrays[array][at, :, n * span : (n + 1) * span]
            if n != SINE_TILE // 2:
                return value
            return jnp.concatenate([value[:, :NKB] + unit, value[:, NKB:]], axis=1)

        sums = [jnp.zeros((NSEP, 8, NKB), jnp.float32) for _ in range(2)]
        position = 0
        for turn, (center, pair) in enumerate(groups):
            e = chosen.at[turn % 2]
            for o in range(len(pair)):
                block = bins[position + o]
                for t in range(NSEP):
                    e[t * per_cell : (t + 1) * per_cell, o * per_cell : (o + 1) * per_cell] = (
                        jnp.where(block == jnp.bfloat16(t), jnp.bfloat16(1), jnp.bfloat16(0))
                    )
            position += len(pair)
            others = [edge[1] if center != edge[1] else edge[2] for edge in pair]
            onehot = e[:, : len(pair) * per_cell]
            for n in range(length // span):
                right = jnp.concatenate([columns(other, n) for other in others], axis=0)
                mixed = jnp.dot(onehot, right, preferred_element_type=jnp.float32)
                left = columns(center, n).astype(jnp.float32)
                term = mixed.reshape(NSEP, per_cell, span) * left[None]
                term = term.reshape(NSEP, per_cell // 8, 8, span).sum(axis=1)
                for s in (0, 1):
                    which = int(2 * n + s == SINE_TILE)
                    sums[which] = sums[which] + term[:, :, s * NKB : (s + 1) * NKB]
        if not last:
            for which in (0, 1):
                out[which] = sums[which]
            return
        for partial in partials:
            sums = [sums[which] + partial[which] for which in (0, 1)]
        first = lax.broadcasted_iota(jnp.int32, (NSEP, 8, NKB), 2) == 0
        out[:NSEP] = (sums[0] + jnp.where(first, 0.0, sums[1])).sum(axis=1)
        counts = jnp.where(first, sums[1], 0.0).sum(axis=1).sum(axis=1, keepdims=True)
        out[NSEP:] = jnp.broadcast_to(counts, (NSEP, NKB))

    shape = (2 * NSEP, NKB) if last else (2, NSEP, 8, NKB)
    n_edges = sum(len(group[1]) for group in groups)
    return pl.pallas_call(
        kernel,
        name=name,
        out_shape=jax.ShapeDtypeStruct(shape, jnp.float32),
        in_specs=vmem(n_arrays + 1 + n_partials),
        out_specs=pl.BlockSpec(memory_space=pltpu.VMEM),
        scratch_shapes=[pltpu.VMEM((2, NSEP * per_cell, 2 * per_cell), jnp.bfloat16)],
        compiler_params=params(24),
        cost_estimate=cost(2 * NSEP * per_cell * per_cell * length * n_edges, 2**20),
    )(*arrays, bins, *partials)


def over_mesh(value, axes):
    for axis in axes:
        count = lax.axis_size(axis)
        if count & (count - 1):
            value = lax.psum(value, axis)
            continue
        step = 1
        while step < count:
            value = value + lax.ppermute(value, axis, [(i, i ^ step) for i in range(count)])
            step *= 2
    return value


def shifted(value, axis, steps):
    count = lax.axis_size(axis)
    return lax.ppermute(
        value, axis, [(i + steps, i) for i in range(count) if 0 <= i + steps < count]
    )


def per_device(forests, resolution, pixel_range, block_pairs, block_count, separation_bin):
    rows, cols, per_cell, length = forests.shape
    stages = plan(rows, cols)
    table = dft_table(length, NKB)
    block = 4 * NKB
    basis = jnp.asarray(
        np.ascontiguousarray(table.reshape(length, length // block, block).transpose(1, 0, 2))
    )
    ends, middle = first_row(forests, pixel_range, resolution, basis)
    above_ends = shifted(ends, "ra", 1)
    above_middle = shifted(middle, "ra", 1)
    own, low, high, *bins = other_rows(
        forests,
        pixel_range,
        resolution,
        basis,
        ends,
        block_pairs,
        block_count,
        separation_bin[0, 0],
        stages,
    )
    right = shifted(low, "dec", 1)
    left = shifted(high, "dec", -1)

    place = {(0, 0): (0, 0), (0, cols - 1): (0, 1)}
    place |= {(0, c): (1, c - 1) for c in range(1, cols - 1)}
    place |= {(r, c): (2, (r - 1) * cols + c) for r in range(1, rows) for c in range(cols)}
    place |= {(r, cols): (3, r) for r in range(rows)}
    place |= {(r, -1): (4, r - 1) for r in range(1, rows)}
    place |= {(rows, 0): (5, 0), (rows, cols - 1): (5, 1)}
    place |= {(rows, c): (6, c - 1) for c in range(1, cols - 1)}
    place |= {(rows, cols): (7, 0), (rows, -1): (8, 0)}

    arrays = [ends, middle, own, right, left, above_ends, above_middle]
    partials = []
    for stage, groups in enumerate(stages):
        if stage == 1:
            above_ends, partials[0] = lax.optimization_barrier((above_ends, partials[0]))
            arrays[5] = above_ends
            arrays.append(shifted(above_ends[:1], "dec", 1))
            arrays.append(shifted(above_ends[1:], "dec", -1))
        named = sorted({place[cell][0] for _, pair in groups for edge in pair for cell in edge[1:3]})
        local = {cell: (named.index(a), i) for cell, (a, i) in place.items() if a in named}
        partials.append(
            pair_sums(
                f"pairs_{stage}",
                groups,
                bins[stage],
                [arrays[i] for i in named],
                local,
                partials if stage == len(stages) - 1 else [],
                stage == len(stages) - 1,
            )
        )
    result = partials[-1]
    tile_power = (result[:NSEP] / (per_cell * length)).reshape(1, 1, NSEP, NKB)
    total = over_mesh(result, ("dec", "ra"))
    sky_power = total[:NSEP] / jnp.maximum(total[NSEP:], 1.0)
    return tile_power, sky_power


def solution(mesh):
    in_specs = (
        P("ra", "dec", None, None),
        P("ra", "dec", None),
        P("ra", "dec", None, None),
        P("ra", "dec", None, None),
        P("ra", "dec"),
        P("ra", "dec", None, None, None),
    )
    out_specs = (P("ra", "dec", None, None), P())
    return jax.shard_map(
        per_device, mesh=mesh, in_specs=in_specs, out_specs=out_specs, check_vma=False
    )
```

```python
import jax
import jax.numpy as jnp
import numpy as np
from jax import lax
from jax.experimental import pallas as pl
from jax.experimental.pallas import tpu as pltpu
from jax.sharding import PartitionSpec as P

NSEP = 8
NKB = 128
VMEM_LIMIT = 32 * 2**20
OFFSETS = ((0, 0), (0, 1), (1, -1), (1, 0), (1, 1))

SINE_TILE = 2


def dft_table(length, n_bins):
    per_bin = length // 2 // n_bins
    sample = np.arange(length // 2)[:, None]
    blocks = []
    for q in range(0, per_bin, 2):
        modes = [np.arange(n_bins)[None, :] * per_bin + q + s for s in (0, 1)]
        angles = [2.0 * np.pi * (sample * mode % length) / length for mode in modes]
        tiles = [np.cos(angle) for angle in angles] + [np.sin(angle) for angle in angles]
        blocks.append(np.concatenate(tiles, axis=1))
    return np.stack(blocks).astype(np.float32).astype(jnp.bfloat16)


def pair_up(edges):
    at = {}
    for edge in edges:
        for cell in {edge[1], edge[2]}:
            at.setdefault(cell, []).append(edge)
    seen, used, groups, rest = set(), set(), [], []

    def visit(cell, up):
        seen.add(cell)
        pending = []
        for edge in at[cell]:
            if edge in used or edge is up:
                continue
            other = edge[2] if edge[1] == cell else edge[1]
            used.add(edge)
            if other == cell or other in seen or not visit(other, edge):
                pending.append(edge)
        pending.sort(key=lambda edge: edge[3])
        taken = len(pending) % 2 == 1 and up is not None
        if taken:
            pending.append(up)
        elif len(pending) % 2:
            rest.append(pending.pop())
        for i in range(0, len(pending), 2):
            groups.append((cell, pending[i : i + 2]))
        return taken

    for cell in sorted(at, reverse=True):
        if cell not in seen:
            visit(cell, None)
    return groups, rest


def plan(rows, cols):
    def arrival(cell):
        r, c = cell
        if r == rows:
            return 1 if c in (0, cols - 1) else 2
        return 0 if c < cols else 1

    edges, handed = [], []
    for r in range(rows):
        for c in range(cols):
            for d, (up, side) in enumerate(OFFSETS):
                a, b = (r, c), (r + up, c + side)
                key = (r * cols + c) * len(OFFSETS) + d
                if b[1] < 0:
                    handed.append(key)
                else:
                    edges.append((key, a, b, max(arrival(a), arrival(b))))
    stages = [[], [], []]
    groups, rest = pair_up([edge for edge in edges if edge[3] < 2])
    for group in groups:
        stages[max(edge[3] for edge in group[1])].append(group)
    groups, rest = pair_up(rest + [edge for edge in edges if edge[3] == 2])
    stages[2] = groups + [(edge[1], [edge]) for edge in rest]
    return stages, handed


def binned(sums, first):
    return (sums[0] + jnp.where(first, 0.0, sums[1])).sum(axis=1)


class Spectra:
    def __init__(self, cells, forests, basis, ranges, widths, scratch):
        (self.flux, self.table, self.masked, self.ranges, self.widths, sems, more_sems) = scratch
        self.cells = cells
        self.flux_copies = [
            pltpu.make_async_copy(forests.at[r, c], self.flux.at[i], sems.at[i])
            for i, (r, c) in enumerate(cells)
        ]
        self.form_copies = [
            pltpu.make_async_copy(ranges, self.ranges, more_sems.at[0]),
            pltpu.make_async_copy(widths, self.widths, more_sems.at[1]),
        ]
        self.table_copies = [
            pltpu.make_async_copy(basis.at[i], self.table.at[i], more_sems.at[2 + i])
            for i in range(basis.shape[0])
        ]

    def start(self):
        for copy in self.form_copies + self.flux_copies + self.table_copies:
            copy.start()

    def mask(self):
        count, per_cell, length = self.flux.shape
        for copy in self.form_copies:
            copy.wait()
        rows = []
        for r, c in self.cells:
            rows += [self.ranges[r, c].astype(jnp.float32), self.widths[r, c : c + 1]]
        filler = -3 * count % 8
        if filler:
            rows.append(jnp.zeros((filler, per_cell), jnp.float32))
        columns = jnp.concatenate(rows, axis=0).T
        step = 16
        position = lax.broadcasted_iota(jnp.int32, (step, length), 1).astype(jnp.float32)
        self.width = []
        for i in range(count):
            low, high, width = (columns[:, 3 * i + j : 3 * i + j + 1] for j in range(3))
            self.width.append(width)
            self.flux_copies[i].wait()
            for row in range(0, per_cell, step):
                inside = (position >= low[row : row + step]) & (position < high[row : row + step])
                kept = jnp.where(inside, self.flux[i, row : row + step].astype(jnp.float32), 0.0)
                start = i * per_cell + row
                self.masked[start : start + step] = kept.astype(jnp.bfloat16)

    def half(self, index, stores):
        _, per_cell, length = self.flux.shape
        per_bin = length // 2 // NKB
        lane = lax.broadcasted_iota(jnp.int32, (1, NKB), 1) * per_bin
        waves = [
            (lane + q).astype(jnp.float32) * (2.0 * jnp.pi / length)
            for q in (2 * index, 2 * index + 1)
        ]
        table = self.table[index]
        tiles = [table[:, i * NKB : (i + 1) * NKB] for i in range(4)]
        later = jnp.concatenate([tiles[0], -tiles[1], tiles[2], -tiles[3]], axis=1)
        raw = jnp.dot(
            self.masked[...],
            jnp.concatenate([table, later], axis=0),
            preferred_element_type=jnp.float32,
        )
        for i in range(len(self.cells)):
            windows = [jnp.exp(-0.5 * (wave * self.width[i]) ** 2) for wave in waves]
            for tile in range(4):
                part = raw[i * per_cell : (i + 1) * per_cell, tile * NKB : (tile + 1) * NKB]
                value = (part * windows[tile % 2]).astype(jnp.bfloat16)
                start = (4 * index + tile) * NKB
                for ref, row in stores[i]:
                    ref[row : row + per_cell, start : start + NKB] = value


def spectra_scratch(count, per_cell, basis, ranges, widths):
    halves, _, _ = basis.shape
    length = 2 * basis.shape[1]
    return [
        pltpu.VMEM((count, per_cell, length), jnp.bfloat16),
        pltpu.VMEM(basis.shape, jnp.bfloat16),
        pltpu.VMEM((count * per_cell, length), jnp.bfloat16),
        pltpu.VMEM(ranges.shape, jnp.int32),
        pltpu.VMEM(widths.shape, jnp.float32),
        pltpu.SemaphoreType.DMA((count,)),
        pltpu.SemaphoreType.DMA((2 + halves,)),
    ]


def vmem(n):
    return [pl.BlockSpec(memory_space=pltpu.VMEM)] * n


def in_hbm(value):
    return pltpu.with_memory_space_constraint(value, pltpu.HBM)


def params():
    return pltpu.CompilerParams(vmem_limit_bytes=VMEM_LIMIT)


def cost(flops, nbytes):
    return pl.CostEstimate(flops=int(flops), bytes_accessed=int(nbytes), transcendentals=0)


def first_row(forests, ranges, widths, basis):
    _, cols, per_cell, length = forests.shape

    def kernel(forests, ranges, widths, basis, ends, middle, *scratch):
        cells = [(0, c) for c in range(cols)]
        spectra = Spectra(cells, forests, basis, ranges, widths, scratch)
        spectra.start()
        spectra.mask()
        stores = [[(ends, 0)]] + [[(middle, i * per_cell)] for i in range(cols - 2)]
        stores.append([(ends, per_cell)])
        for index in range(basis.shape[0]):
            spectra.table_copies[index].wait()
            spectra.half(index, stores)

    return pl.pallas_call(
        kernel,
        name="first_row",
        out_shape=[
            jax.ShapeDtypeStruct((n * per_cell, length), jnp.bfloat16) for n in (2, cols - 2)
        ],
        in_specs=[pl.BlockSpec(memory_space=pltpu.HBM)] * 4,
        out_specs=vmem(2),
        scratch_shapes=spectra_scratch(cols, per_cell, basis, ranges, widths),
        compiler_params=params(),
        cost_estimate=cost(2 * cols * per_cell * length * length, 5 * 2**20),
    )(in_hbm(forests), in_hbm(ranges), in_hbm(widths), in_hbm(basis))


def other_rows(forests, ranges, widths, basis, ends, entries, bins, stages, handed):
    rows, cols, per_cell, length = forests.shape
    slots = bins.shape[0]
    cells = [(r, c) for r in range(1, rows) for c in range(cols)]
    sizes = [sum(len(group[1]) for group in stage) for stage in stages]
    strip = per_cell * per_cell // length
    n_basis = basis.shape[0]

    def kernel(*refs):
        forests, ranges, widths, basis, ends, entries, bins = refs[:7]
        own, low, counts = refs[7:10]
        sorted_bins, scratch = refs[10 : 10 + len(stages)], refs[10 + len(stages) :]
        entries_here, slot_of, list_sem = scratch[-3:]
        list_copy = pltpu.make_async_copy(entries, entries_here, list_sem)
        list_copy.start()
        spectra = Spectra(cells, forests, basis, ranges, widths, scratch[:-3])
        spectra.start()
        list_copy.wait()

        @pl.loop(0, slots)
        def _(s):
            cell, up, side, live = (entries_here[0, i, 0, s] for i in range(4))
            slot_of[cell * len(OFFSETS) + 3 * up + side] = jnp.where(s < live, s, s + slots)

        def bins_of(key):
            at = slot_of[key]
            dead = at >= slots
            block = bins[jnp.where(dead, at - slots, at)].astype(jnp.float32)
            return block + jnp.where(dead, float(NSEP), 0.0)

        spectra.mask()
        low[:per_cell] = ends[:per_cell]
        stores = []
        for i, (r, c) in enumerate(cells):
            stores.append([(own, i * per_cell)])
            if c == 0:
                stores[-1].append((low, r * per_cell))
        for index in range(n_basis):
            spectra.table_copies[index].wait()
            spectra.half(index, stores)
        for target, stage in zip(sorted_bins, stages):
            for i, (center, edge) in enumerate((c, edge) for c, pair in stage for edge in pair):
                block = bins_of(edge[0])
                target[i] = (block if center == edge[1] else block.T).astype(jnp.bfloat16)
        found = [jnp.zeros((8, per_cell), jnp.float32) for _ in range(NSEP)]
        for r, key in enumerate(handed):
            block = bins_of(key)
            for t in range(NSEP):
                one = jnp.where(block == float(t), 1.0, 0.0)
                found[t] = found[t] + one.reshape(per_cell // 8, 8, per_cell).sum(axis=0)
            block = block.astype(jnp.bfloat16)
            start = rows * per_cell + r * strip
            for i in range(per_cell // strip):
                low[start : start + strip, i * per_cell : (i + 1) * per_cell] = (
                    block[i * strip : (i + 1) * strip]
                )
        for t in range(NSEP):
            counts[t] = found[t]

    hbm, anywhere = (pl.BlockSpec(memory_space=space) for space in (pltpu.HBM, pl.ANY))
    bf16, f32 = jnp.bfloat16, jnp.float32
    shapes = [((rows - 1) * cols * per_cell, length), (rows * (per_cell + strip), length)]
    shapes = [jax.ShapeDtypeStruct(shape, bf16) for shape in shapes]
    shapes.append(jax.ShapeDtypeStruct((NSEP, 8, per_cell), f32))
    shapes += [jax.ShapeDtypeStruct((size, per_cell, per_cell), bf16) for size in sizes]
    return pl.pallas_call(
        kernel,
        name="other_rows",
        out_shape=shapes,
        in_specs=[hbm] * 4 + vmem(1) + [anywhere] + vmem(1),
        out_specs=vmem(len(shapes)),
        scratch_shapes=spectra_scratch(len(cells), per_cell, basis, ranges, widths)
        + [
            pltpu.SMEM(entries.shape, jnp.int32),
            pltpu.SMEM((slots,), jnp.int32),
            pltpu.SemaphoreType.DMA,
        ],
        compiler_params=params(),
        cost_estimate=cost(2 * len(cells) * per_cell * length * length, 8 * 2**20),
    )(
        in_hbm(forests),
        in_hbm(ranges),
        in_hbm(widths),
        in_hbm(basis),
        ends,
        entries,
        bins,
    )


def pair_sums(groups, given, bins, arrays, place, carried, per_cell, last):
    length = arrays[0].shape[1]
    n_arrays, n_carried = len(arrays), len(carried)
    span = 2 * NKB
    strip = per_cell * per_cell // length

    def kernel(*refs):
        arrays, bins = refs[:n_arrays], refs[n_arrays]
        carried = refs[n_arrays + 1 : n_arrays + 1 + n_carried]
        outs, chosen = refs[n_arrays + 1 + n_carried : -1], refs[-1]
        lane = lax.broadcasted_iota(jnp.int32, (per_cell, NKB), 1)
        unit = jnp.where(lane == 0, 1.0, 0.0).astype(jnp.bfloat16)
        first = lax.broadcasted_iota(jnp.int32, (NSEP, 8, NKB), 2) == 0

        def columns(cell, n):
            array, row = place[cell]
            value = arrays[array][row : row + per_cell, n * span : (n + 1) * span]
            if n != SINE_TILE // 2:
                return value
            return jnp.concatenate([value[:, :NKB] + unit, value[:, NKB:]], axis=1)

        def choose(e, block, row, column):
            for t in range(NSEP):
                start = t * per_cell + row
                e[start : start + block.shape[0], column : column + per_cell] = jnp.where(
                    block == jnp.bfloat16(t), jnp.bfloat16(1), jnp.bfloat16(0)
                )

        def add(sums, e, center, others):
            onehot = e[:, : len(others) * per_cell]
            for n in range(length // span):
                right = jnp.concatenate([columns(other, n) for other in others], axis=0)
                mixed = jnp.dot(onehot, right, preferred_element_type=jnp.float32)
                left = columns(center, n).astype(jnp.float32)
                term = mixed.reshape(NSEP, per_cell, span) * left[None]
                term = term.reshape(NSEP, per_cell // 8, 8, span).sum(axis=1)
                for s in (0, 1):
                    which = int(2 * n + s == SINE_TILE)
                    sums[which] = sums[which] + term[:, :, s * NKB : (s + 1) * NKB]

        def zeros():
            return [jnp.zeros((NSEP, 8, NKB), jnp.float32) for _ in range(2)]

        sums, others_sums = zeros(), zeros()
        position = turn = 0
        for center, pair in groups:
            e = chosen.at[turn % 2]
            turn += 1
            for o in range(len(pair)):
                choose(e, bins[position + o], 0, o * per_cell)
            position += len(pair)
            add(sums, e, center, [edge[1] if center != edge[1] else edge[2] for edge in pair])
        for array, start, a, b in given:
            e = chosen.at[turn % 2]
            turn += 1
            for i in range(per_cell // strip):
                piece = arrays[array][start : start + strip, i * per_cell : (i + 1) * per_cell]
                choose(e, piece, i * strip, 0)
            add(others_sums, e, a, [b])
        if not last:
            for which in (0, 1):
                outs[0][which] = sums[which]
            if given:
                outs[1][...] = binned(others_sums, first)
            return
        *partials, left_out, for_others = carried
        for partial in partials:
            sums = [sums[which] + partial[which] for which in (0, 1)]
        own = binned(sums, first)
        outs[0][...] = own
        outs[1][:NSEP] = own + for_others[...]
        counts = (jnp.where(first, sums[1], 0.0) + left_out[...]).sum(axis=1)
        outs[1][NSEP:] = jnp.broadcast_to(counts.sum(axis=1, keepdims=True), (NSEP, NKB))

    if last:
        shapes = [(NSEP, NKB), (2 * NSEP, NKB)]
    else:
        shapes = [(2, NSEP, 8, NKB)] + [(NSEP, NKB)] * bool(given)
    n_edges = sum(len(group[1]) for group in groups) + len(given)
    return pl.pallas_call(
        kernel,
        out_shape=[jax.ShapeDtypeStruct(shape, jnp.float32) for shape in shapes],
        in_specs=vmem(n_arrays + 1 + n_carried),
        out_specs=vmem(len(shapes)),
        scratch_shapes=[pltpu.VMEM((2, NSEP * per_cell, 2 * per_cell), jnp.bfloat16)],
        compiler_params=params(),
        cost_estimate=cost(2 * NSEP * per_cell * per_cell * length * n_edges, 2**20),
    )(*arrays, bins, *carried)


def over_mesh(value, axes):
    for axis in axes:
        count = lax.axis_size(axis)
        if count & (count - 1):
            value = lax.psum(value, axis)
            continue
        step = 1
        while step < count:
            value = value + lax.ppermute(value, axis, [(i, i ^ step) for i in range(count)])
            step *= 2
    return value


def shifted(value, axis, steps):
    count = lax.axis_size(axis)
    return lax.ppermute(
        value, axis, [(i + steps, i) for i in range(count) if 0 <= i + steps < count]
    )


def per_device(forests, resolution, pixel_range, block_pairs, block_count, separation_bin):
    rows, cols, per_cell, length = forests.shape
    stages, handed = plan(rows, cols)
    table = dft_table(length, NKB)
    basis = jnp.asarray(table)
    live = jnp.broadcast_to(block_count[..., None, None], (1, 1, 1, block_pairs.shape[2]))
    entries = jnp.concatenate([block_pairs.transpose(0, 3, 1, 2), live], axis=1)
    ends, middle = first_row(forests, pixel_range, resolution, basis)
    above_ends = shifted(ends, "ra", 1)
    above_middle = shifted(middle, "ra", 1)
    own, low, counts, *bins = other_rows(
        forests,
        pixel_range,
        resolution,
        basis,
        ends,
        entries,
        separation_bin[0, 0],
        stages,
        handed,
    )
    right = shifted(low, "dec", 1)

    place = {(0, 0): (0, 0), (0, cols - 1): (0, 1)}
    place |= {(0, c): (1, c - 1) for c in range(1, cols - 1)}
    place |= {(r, c): (2, (r - 1) * cols + c) for r in range(1, rows) for c in range(cols)}
    place |= {(r, cols): (3, r) for r in range(rows)}
    place |= {(rows, 0): (4, 0), (rows, cols - 1): (4, 1)}
    place |= {(rows, c): (5, c - 1) for c in range(1, cols - 1)}
    place |= {(rows, cols): (6, 0)}
    strip = per_cell * per_cell // length
    given = [(3, rows * per_cell + r * strip, (r, cols), (r + 1, cols - 1)) for r in range(rows)]

    def sums(stage, arrays, given, carried):
        cells = {cell for _, pair in stages[stage] for edge in pair for cell in edge[1:3]}
        cells |= {cell for one in given for cell in one[2:]}
        named = sorted({place[cell][0] for cell in cells})
        local = {cell: (named.index(place[cell][0]), place[cell][1] * per_cell) for cell in cells}
        return pair_sums(
            stages[stage],
            [(named.index(one[0]), *one[1:]) for one in given],
            bins[stage],
            [arrays[i] for i in named],
            local,
            carried,
            per_cell,
            stage == len(stages) - 1,
        )

    arrays = [ends, middle, own, right, above_ends, above_middle]
    (partial,) = sums(0, arrays, [], [])
    above_ends, partial = lax.optimization_barrier((above_ends, partial))
    arrays[4] = above_ends
    arrays.append(shifted(above_ends[:per_cell], "dec", 1))
    partial_too, for_others = sums(1, arrays, given, [])
    from_left = shifted(for_others, "dec", -1)
    own_sums, result = sums(2, arrays, [], [partial, partial_too, counts, for_others])
    tile_power = ((own_sums + from_left) / (per_cell * length)).reshape(1, 1, NSEP, NKB)
    total = over_mesh(result, ("dec", "ra"))
    sky_power = total[:NSEP] / jnp.maximum(total[NSEP:], 1.0)
    return tile_power, sky_power


def solution(mesh):
    in_specs = (
        P("ra", "dec", None, None),
        P("ra", "dec", None),
        P("ra", "dec", None, None),
        P("ra", "dec", None, None),
        P("ra", "dec"),
        P("ra", "dec", None, None, None),
    )
    out_specs = (P("ra", "dec", None, None), P())
    return jax.shard_map(
        per_device, mesh=mesh, in_specs=in_specs, out_specs=out_specs, check_vma=False
    )
```

```python
import jax
import jax.numpy as jnp
import numpy as np
from jax import lax
from jax.experimental import pallas as pl
from jax.experimental.pallas import tpu as pltpu
from jax.sharding import PartitionSpec as P

NSEP = 8
NKB = 128
VMEM_LIMIT = 32 * 2**20
OFFSETS = ((0, 0), (0, 1), (1, -1), (1, 0), (1, 1))

SINE_TILE = 2


def dft_table(length, n_bins):
    per_bin = length // 2 // n_bins
    sample = np.arange(length // 2)[:, None]
    blocks = []
    for q in range(0, per_bin, 2):
        modes = [np.arange(n_bins)[None, :] * per_bin + q + s for s in (0, 1)]
        angles = [2.0 * np.pi * (sample * mode % length) / length for mode in modes]
        tiles = [np.cos(angle) for angle in angles] + [np.sin(angle) for angle in angles]
        blocks.append(np.concatenate(tiles, axis=1))
    return np.stack(blocks).astype(np.float32).astype(jnp.bfloat16)


def pair_up(edges):
    at = {}
    for edge in edges:
        for cell in {edge[1], edge[2]}:
            at.setdefault(cell, []).append(edge)
    seen, used, groups, rest = set(), set(), [], []

    def visit(cell, up):
        seen.add(cell)
        pending = []
        for edge in at[cell]:
            if edge in used or edge is up:
                continue
            other = edge[2] if edge[1] == cell else edge[1]
            used.add(edge)
            if other == cell or other in seen or not visit(other, edge):
                pending.append(edge)
        pending.sort(key=lambda edge: edge[3])
        taken = len(pending) % 2 == 1 and up is not None
        if taken:
            pending.append(up)
        elif len(pending) % 2:
            rest.append(pending.pop())
        for i in range(0, len(pending), 2):
            groups.append((cell, pending[i : i + 2]))
        return taken

    for cell in sorted(at, reverse=True):
        if cell not in seen:
            visit(cell, None)
    return groups, rest


def plan(rows, cols):
    def arrival(cell):
        r, c = cell
        if r == rows:
            return 1 if c in (0, cols - 1) else 2
        return 0 if c < cols else 1

    edges, handed = [], []
    for r in range(rows):
        for c in range(cols):
            for d, (up, side) in enumerate(OFFSETS):
                a, b = (r, c), (r + up, c + side)
                key = (r * cols + c) * len(OFFSETS) + d
                if b[1] < 0:
                    handed.append(key)
                else:
                    edges.append((key, a, b, max(arrival(a), arrival(b))))
    stages = [[], [], []]
    groups, rest = pair_up([edge for edge in edges if edge[3] < 2])
    for group in groups:
        stages[max(edge[3] for edge in group[1])].append(group)
    groups, rest = pair_up(rest + [edge for edge in edges if edge[3] == 2])
    stages[2] = groups + [(edge[1], [edge]) for edge in rest]
    return stages, handed


def binned(sums, first):
    return (sums[0] + jnp.where(first, 0.0, sums[1])).sum(axis=1)


class Spectra:
    def __init__(self, cells, forests, basis, ranges, widths, scratch):
        (self.flux, self.table, self.masked, self.ranges, self.widths, sems, more_sems) = scratch
        self.cells = cells
        self.flux_copies = [
            pltpu.make_async_copy(forests.at[r, c], self.flux.at[i], sems.at[i])
            for i, (r, c) in enumerate(cells)
        ]
        self.form_copies = [
            pltpu.make_async_copy(ranges, self.ranges, more_sems.at[0]),
            pltpu.make_async_copy(widths, self.widths, more_sems.at[1]),
        ]
        self.table_copies = [
            pltpu.make_async_copy(basis.at[i], self.table.at[i], more_sems.at[2 + i])
            for i in range(basis.shape[0])
        ]

    def start(self):
        for copy in self.form_copies + self.flux_copies + self.table_copies:
            copy.start()

    def mask(self):
        count, per_cell, length = self.flux.shape
        for copy in self.form_copies:
            copy.wait()
        rows = []
        for r, c in self.cells:
            rows += [self.ranges[r, c].astype(jnp.float32), self.widths[r, c : c + 1]]
        filler = -3 * count % 8
        if filler:
            rows.append(jnp.zeros((filler, per_cell), jnp.float32))
        columns = jnp.concatenate(rows, axis=0).T
        step = 16
        position = lax.broadcasted_iota(jnp.int32, (step, length), 1).astype(jnp.float32)
        self.width = []
        for i in range(count):
            low, high, width = (columns[:, 3 * i + j : 3 * i + j + 1] for j in range(3))
            self.width.append(width)
            self.flux_copies[i].wait()
            for row in range(0, per_cell, step):
                inside = (position >= low[row : row + step]) & (position < high[row : row + step])
                kept = jnp.where(inside, self.flux[i, row : row + step].astype(jnp.float32), 0.0)
                start = i * per_cell + row
                self.masked[start : start + step] = kept.astype(jnp.bfloat16)

    def half(self, index, stores):
        _, per_cell, length = self.flux.shape
        per_bin = length // 2 // NKB
        lane = lax.broadcasted_iota(jnp.int32, (1, NKB), 1) * per_bin
        waves = [
            (lane + q).astype(jnp.float32) * (2.0 * jnp.pi / length)
            for q in (2 * index, 2 * index + 1)
        ]
        table = self.table[index]
        tiles = [table[:, i * NKB : (i + 1) * NKB] for i in range(4)]
        later = jnp.concatenate([tiles[0], -tiles[1], tiles[2], -tiles[3]], axis=1)
        raw = jnp.dot(
            self.masked[...],
            jnp.concatenate([table, later], axis=0),
            preferred_element_type=jnp.float32,
        )
        for i in range(len(self.cells)):
            windows = [jnp.exp(-0.5 * (wave * self.width[i]) ** 2) for wave in waves]
            for tile in range(4):
                part = raw[i * per_cell : (i + 1) * per_cell, tile * NKB : (tile + 1) * NKB]
                value = (part * windows[tile % 2]).astype(jnp.bfloat16)
                start = (4 * index + tile) * NKB
                for ref, row in stores[i]:
                    ref[row : row + per_cell, start : start + NKB] = value


def spectra_scratch(count, per_cell, basis, ranges, widths):
    halves, _, _ = basis.shape
    length = 2 * basis.shape[1]
    return [
        pltpu.VMEM((count, per_cell, length), jnp.bfloat16),
        pltpu.VMEM(basis.shape, jnp.bfloat16),
        pltpu.VMEM((count * per_cell, length), jnp.bfloat16),
        pltpu.VMEM(ranges.shape, jnp.int32),
        pltpu.VMEM(widths.shape, jnp.float32),
        pltpu.SemaphoreType.DMA((count,)),
        pltpu.SemaphoreType.DMA((2 + halves,)),
    ]


def vmem(n):
    return [pl.BlockSpec(memory_space=pltpu.VMEM)] * n


def in_hbm(value):
    return pltpu.with_memory_space_constraint(value, pltpu.HBM)


def params():
    return pltpu.CompilerParams(vmem_limit_bytes=VMEM_LIMIT)


def cost(flops, nbytes):
    return pl.CostEstimate(flops=int(flops), bytes_accessed=int(nbytes), transcendentals=0)


def end_cells(forests, ranges, widths, basis):
    _, cols, per_cell, length = forests.shape
    cells = [(0, 0), (0, cols - 1)]

    def kernel(forests, ranges, widths, basis, ends, *scratch):
        spectra = Spectra(cells, forests, basis, ranges, widths, scratch)
        spectra.start()
        spectra.mask()
        for copy in spectra.table_copies:
            copy.wait()
        for index in range(basis.shape[0]):
            spectra.half(index, [[(ends, 0)], [(ends, per_cell)]])

    return pl.pallas_call(
        kernel,
        name="end_cells",
        out_shape=jax.ShapeDtypeStruct((2 * per_cell, length), jnp.bfloat16),
        in_specs=[pl.BlockSpec(memory_space=pltpu.HBM)] * 4,
        out_specs=pl.BlockSpec(memory_space=pltpu.VMEM),
        scratch_shapes=spectra_scratch(2, per_cell, basis, ranges, widths),
        compiler_params=params(),
        cost_estimate=cost(4 * per_cell * length * length, 4 * 2**20),
    )(in_hbm(forests), in_hbm(ranges), in_hbm(widths), in_hbm(basis))


def other_cells(forests, ranges, widths, basis, ends, entries, bins, stages, handed):
    rows, cols, per_cell, length = forests.shape
    slots = bins.shape[0]
    cells = [(0, c) for c in range(1, cols - 1)]
    cells += [(r, c) for r in range(1, rows) for c in range(cols)]
    sizes = [sum(len(group[1]) for group in stage) for stage in stages]
    strip = per_cell * per_cell // length
    n_basis = basis.shape[0]

    def kernel(*refs):
        forests, ranges, widths, basis, ends, entries, bins = refs[:7]
        middle, own, low, counts = refs[7:11]
        sorted_bins, scratch = refs[11 : 11 + len(stages)], refs[11 + len(stages) :]
        entries_here, slot_of, list_sem = scratch[-3:]
        list_copy = pltpu.make_async_copy(entries, entries_here, list_sem)
        list_copy.start()
        spectra = Spectra(cells, forests, basis, ranges, widths, scratch[:-3])
        spectra.start()
        list_copy.wait()

        @pl.loop(0, slots)
        def _(s):
            cell, up, side, live = (entries_here[0, i, 0, s] for i in range(4))
            slot_of[cell * len(OFFSETS) + 3 * up + side] = jnp.where(live > 0, s, s + slots)

        def bins_of(key):
            at = slot_of[key]
            dead = at >= slots
            block = bins[jnp.where(dead, at - slots, at)].astype(jnp.float32)
            return block + jnp.where(dead, float(NSEP), 0.0)

        spectra.mask()
        low[:per_cell] = ends[:per_cell]
        stores = []
        for r, c in cells:
            if r == 0:
                stores.append([(middle, (c - 1) * per_cell)])
                continue
            stores.append([(own, ((r - 1) * cols + c) * per_cell)])
            if c == 0:
                stores[-1].append((low, r * per_cell))
        for copy in spectra.table_copies:
            copy.wait()
        for index in range(n_basis):
            spectra.half(index, stores)
        for target, stage in zip(sorted_bins, stages):
            for i, (center, edge) in enumerate((c, edge) for c, pair in stage for edge in pair):
                block = bins_of(edge[0])
                target[i] = (block if center == edge[1] else block.T).astype(jnp.bfloat16)
        found = [jnp.zeros((8, per_cell), jnp.float32) for _ in range(NSEP)]
        for r, key in enumerate(handed):
            block = bins_of(key)
            for t in range(NSEP):
                one = jnp.where(block == float(t), 1.0, 0.0)
                found[t] = found[t] + one.reshape(per_cell // 8, 8, per_cell).sum(axis=0)
            block = block.astype(jnp.bfloat16)
            start = rows * per_cell + r * strip
            for i in range(per_cell // strip):
                low[start : start + strip, i * per_cell : (i + 1) * per_cell] = (
                    block[i * strip : (i + 1) * strip]
                )
        for t in range(NSEP):
            counts[t] = found[t]

    hbm, anywhere = (pl.BlockSpec(memory_space=space) for space in (pltpu.HBM, pl.ANY))
    bf16, f32 = jnp.bfloat16, jnp.float32
    shapes = [((cols - 2) * per_cell, length), ((rows - 1) * cols * per_cell, length)]
    shapes.append((rows * (per_cell + strip), length))
    shapes = [jax.ShapeDtypeStruct(shape, bf16) for shape in shapes]
    shapes.append(jax.ShapeDtypeStruct((NSEP, 8, per_cell), f32))
    shapes += [jax.ShapeDtypeStruct((size, per_cell, per_cell), bf16) for size in sizes]
    return pl.pallas_call(
        kernel,
        name="other_cells",
        out_shape=shapes,
        in_specs=[hbm] * 4 + vmem(1) + [anywhere] + vmem(1),
        out_specs=vmem(len(shapes)),
        scratch_shapes=spectra_scratch(len(cells), per_cell, basis, ranges, widths)
        + [
            pltpu.SMEM(entries.shape, jnp.int32),
            pltpu.SMEM((slots,), jnp.int32),
            pltpu.SemaphoreType.DMA,
        ],
        compiler_params=params(),
        cost_estimate=cost(2 * len(cells) * per_cell * length * length, 8 * 2**20),
    )(
        in_hbm(forests),
        in_hbm(ranges),
        in_hbm(widths),
        in_hbm(basis),
        ends,
        entries,
        bins,
    )


def pair_sums(groups, given, bins, arrays, place, carried, per_cell, last):
    length = arrays[0].shape[1]
    n_arrays, n_carried = len(arrays), len(carried)
    span = 2 * NKB
    strip = per_cell * per_cell // length

    def kernel(*refs):
        arrays, bins = refs[:n_arrays], refs[n_arrays]
        carried = refs[n_arrays + 1 : n_arrays + 1 + n_carried]
        outs, chosen = refs[n_arrays + 1 + n_carried : -1], refs[-1]
        lane = lax.broadcasted_iota(jnp.int32, (per_cell, NKB), 1)
        unit = jnp.where(lane == 0, 1.0, 0.0).astype(jnp.bfloat16)
        first = lax.broadcasted_iota(jnp.int32, (NSEP, 8, NKB), 2) == 0

        def columns(cell, n):
            array, row = place[cell]
            value = arrays[array][row : row + per_cell, n * span : (n + 1) * span]
            if n != SINE_TILE // 2:
                return value
            return jnp.concatenate([value[:, :NKB] + unit, value[:, NKB:]], axis=1)

        def choose(e, block, row, column):
            for t in range(NSEP):
                start = t * per_cell + row
                e[start : start + block.shape[0], column : column + per_cell] = jnp.where(
                    block == jnp.bfloat16(t), jnp.bfloat16(1), jnp.bfloat16(0)
                )

        def add(sums, e, center, others):
            onehot = e[:, : len(others) * per_cell]
            for n in range(length // span):
                right = jnp.concatenate([columns(other, n) for other in others], axis=0)
                mixed = jnp.dot(onehot, right, preferred_element_type=jnp.float32)
                left = columns(center, n).astype(jnp.float32)
                term = mixed.reshape(NSEP, per_cell, span) * left[None]
                term = term.reshape(NSEP, per_cell // 8, 8, span).sum(axis=1)
                for s in (0, 1):
                    which = int(2 * n + s == SINE_TILE)
                    sums[which] = sums[which] + term[:, :, s * NKB : (s + 1) * NKB]

        def zeros():
            return [jnp.zeros((NSEP, 8, NKB), jnp.float32) for _ in range(2)]

        sums, others_sums = zeros(), zeros()
        position = turn = 0
        for center, pair in groups:
            e = chosen.at[turn % 2]
            turn += 1
            for o in range(len(pair)):
                choose(e, bins[position + o], 0, o * per_cell)
            position += len(pair)
            add(sums, e, center, [edge[1] if center != edge[1] else edge[2] for edge in pair])
        for array, start, a, b in given:
            e = chosen.at[turn % 2]
            turn += 1
            for i in range(per_cell // strip):
                piece = arrays[array][start : start + strip, i * per_cell : (i + 1) * per_cell]
                choose(e, piece, i * strip, 0)
            add(others_sums, e, a, [b])
        if not last:
            for which in (0, 1):
                outs[0][which] = sums[which]
            if given:
                outs[1][...] = binned(others_sums, first)
            return
        *partials, left_out, for_others = carried
        for partial in partials:
            sums = [sums[which] + partial[which] for which in (0, 1)]
        own = binned(sums, first)
        outs[0][...] = own
        outs[1][:NSEP] = own + for_others[...]
        counts = (jnp.where(first, sums[1], 0.0) + left_out[...]).sum(axis=1)
        outs[1][NSEP:] = jnp.broadcast_to(counts.sum(axis=1, keepdims=True), (NSEP, NKB))

    if last:
        shapes = [(NSEP, NKB), (2 * NSEP, NKB)]
    else:
        shapes = [(2, NSEP, 8, NKB)] + [(NSEP, NKB)] * bool(given)
    n_edges = sum(len(group[1]) for group in groups) + len(given)
    return pl.pallas_call(
        kernel,
        out_shape=[jax.ShapeDtypeStruct(shape, jnp.float32) for shape in shapes],
        in_specs=vmem(n_arrays + 1 + n_carried),
        out_specs=vmem(len(shapes)),
        scratch_shapes=[pltpu.VMEM((2, NSEP * per_cell, 2 * per_cell), jnp.bfloat16)],
        compiler_params=params(),
        cost_estimate=cost(2 * NSEP * per_cell * per_cell * length * n_edges, 2**20),
    )(*arrays, bins, *carried)


def over_mesh(value, ra, dec):
    def steps(axis):
        count = lax.axis_size(axis)
        return [1 << i for i in range(count.bit_length() - 1)]

    exchanges = [(ra, step) for step in steps(ra)] + [(dec, step) for step in steps(dec)[::-1]]
    for axis, step in exchanges:
        count = lax.axis_size(axis)
        if count & (count - 1):
            raise ValueError("axis size")
        value = value + lax.ppermute(value, axis, [(i, i ^ step) for i in range(count)])
    return value


def shifted(value, axis, steps):
    count = lax.axis_size(axis)
    return lax.ppermute(
        value, axis, [(i + steps, i) for i in range(count) if 0 <= i + steps < count]
    )


def per_device(forests, resolution, pixel_range, block_pairs, block_count, separation_bin):
    rows, cols, per_cell, length = forests.shape
    stages, handed = plan(rows, cols)
    table = dft_table(length, NKB)
    basis = jnp.asarray(table)
    slot = lax.broadcasted_iota(jnp.int32, (1, 1, 1, block_pairs.shape[2]), 3)
    live = (slot < block_count[..., None, None]).astype(jnp.int32)
    entries = jnp.concatenate([block_pairs.transpose(0, 3, 1, 2), live], axis=1)
    ends = end_cells(forests, pixel_range, resolution, basis)
    above_ends = shifted(ends, "ra", 1)
    middle, own, low, counts, *bins = other_cells(
        forests,
        pixel_range,
        resolution,
        basis,
        ends,
        entries,
        separation_bin[0, 0],
        stages,
        handed,
    )
    above_middle = shifted(middle, "ra", 1)
    right = shifted(low, "dec", 1)

    place = {(0, 0): (0, 0), (0, cols - 1): (0, 1)}
    place |= {(0, c): (1, c - 1) for c in range(1, cols - 1)}
    place |= {(r, c): (2, (r - 1) * cols + c) for r in range(1, rows) for c in range(cols)}
    place |= {(r, cols): (3, r) for r in range(rows)}
    place |= {(rows, 0): (4, 0), (rows, cols - 1): (4, 1)}
    place |= {(rows, c): (5, c - 1) for c in range(1, cols - 1)}
    place |= {(rows, cols): (6, 0)}
    strip = per_cell * per_cell // length
    given = [(3, rows * per_cell + r * strip, (r, cols), (r + 1, cols - 1)) for r in range(rows)]

    def sums(stage, arrays, given, carried):
        cells = {cell for _, pair in stages[stage] for edge in pair for cell in edge[1:3]}
        cells |= {cell for one in given for cell in one[2:]}
        named = sorted({place[cell][0] for cell in cells})
        local = {cell: (named.index(place[cell][0]), place[cell][1] * per_cell) for cell in cells}
        return pair_sums(
            stages[stage],
            [(named.index(one[0]), *one[1:]) for one in given],
            bins[stage],
            [arrays[i] for i in named],
            local,
            carried,
            per_cell,
            stage == len(stages) - 1,
        )

    arrays = [ends, middle, own, right, above_ends, above_middle]
    (partial,) = sums(0, arrays, [], [])
    above_ends, partial = lax.optimization_barrier((above_ends, partial))
    arrays[4] = above_ends
    arrays.append(shifted(above_ends[:per_cell], "dec", 1))
    partial_too, for_others = sums(1, arrays, given, [])
    from_left = shifted(for_others, "dec", -1)
    own_sums, result = sums(2, arrays, [], [partial, partial_too, counts, for_others])
    tile_power = (own_sums + from_left) / (per_cell * length)
    tile_power = tile_power.reshape(1, 1, NSEP, NKB)
    total = over_mesh(result, "ra", "dec")
    sky_power = total[:NSEP] / jnp.maximum(total[NSEP:], 1.0)
    return tile_power, sky_power


def solution(mesh):
    in_specs = (
        P("ra", "dec", None, None),
        P("ra", "dec", None),
        P("ra", "dec", None, None),
        P("ra", "dec", None, None),
        P("ra", "dec"),
        P("ra", "dec", None, None, None),
    )
    out_specs = (P("ra", "dec", None, None), P())
    return jax.shard_map(
        per_device, mesh=mesh, in_specs=in_specs, out_specs=out_specs, check_vma=False
    )
```

```python
import jax
import jax.numpy as jnp
import numpy as np
from jax import lax
from jax.experimental import pallas as pl
from jax.experimental.pallas import tpu as pltpu
from jax.sharding import PartitionSpec as P

NSEP = 8
NKB = 128
VMEM_LIMIT = 32 * 2**20
OFFSETS = ((0, 0), (0, 1), (1, -1), (1, 0), (1, 1))

SINE_TILE = 2


def dft_table(length, n_bins):
    per_bin = length // 2 // n_bins
    sample = np.arange(length // 2)[:, None]
    blocks = []
    for q in range(0, per_bin, 2):
        modes = [np.arange(n_bins)[None, :] * per_bin + q + s for s in (0, 1)]
        angles = [2.0 * np.pi * (sample * mode % length) / length for mode in modes]
        tiles = [np.cos(angle) for angle in angles] + [np.sin(angle) for angle in angles]
        blocks.append(np.concatenate(tiles, axis=1))
    return np.stack(blocks).astype(np.float32).astype(jnp.bfloat16)


def pair_up(edges):
    at = {}
    for edge in edges:
        for cell in {edge[1], edge[2]}:
            at.setdefault(cell, []).append(edge)
    seen, used, groups, rest = set(), set(), [], []

    def visit(cell, up):
        seen.add(cell)
        pending = []
        for edge in at[cell]:
            if edge in used or edge is up:
                continue
            other = edge[2] if edge[1] == cell else edge[1]
            used.add(edge)
            if other == cell or other in seen or not visit(other, edge):
                pending.append(edge)
        pending.sort(key=lambda edge: edge[3])
        taken = len(pending) % 2 == 1 and up is not None
        if taken:
            pending.append(up)
        elif len(pending) % 2:
            rest.append(pending.pop())
        for i in range(0, len(pending), 2):
            groups.append((cell, pending[i : i + 2]))
        return taken

    for cell in sorted(at, reverse=True):
        if cell not in seen:
            visit(cell, None)
    return groups, rest


def plan(rows, cols):
    def arrival(cell):
        r, c = cell
        if r == rows:
            return 1 if c in (0, cols - 1) else 2
        return 0 if c < cols else 1

    edges, handed = [], []
    for r in range(rows):
        for c in range(cols):
            for d, (up, side) in enumerate(OFFSETS):
                a, b = (r, c), (r + up, c + side)
                key = (r * cols + c) * len(OFFSETS) + d
                if b[1] < 0:
                    handed.append(key)
                else:
                    edges.append((key, a, b, max(arrival(a), arrival(b))))
    stages = [[], [], []]
    groups, rest = pair_up([edge for edge in edges if edge[3] < 2])
    for group in groups:
        stages[max(edge[3] for edge in group[1])].append(group)
    groups, rest = pair_up(rest + [edge for edge in edges if edge[3] == 2])
    stages[2] = groups + [(edge[1], [edge]) for edge in rest]
    return stages, handed


def binned(sums, first):
    return (sums[0] + jnp.where(first, 0.0, sums[1])).sum(axis=1)


class Spectra:
    def __init__(self, cells, forests, basis, ranges, widths, scratch):
        (self.flux, self.table, self.masked, self.ranges, self.widths, sems, more_sems) = scratch
        self.cells = cells
        self.flux_copies = [
            pltpu.make_async_copy(forests.at[r, c], self.flux.at[i], sems.at[i])
            for i, (r, c) in enumerate(cells)
        ]
        self.form_copies = [
            pltpu.make_async_copy(ranges, self.ranges, more_sems.at[0]),
            pltpu.make_async_copy(widths, self.widths, more_sems.at[1]),
        ]
        self.table_copies = [
            pltpu.make_async_copy(basis.at[i], self.table.at[i], more_sems.at[2 + i])
            for i in range(basis.shape[0])
        ]

    def start(self):
        for copy in self.form_copies + self.flux_copies + self.table_copies:
            copy.start()

    def mask(self):
        count, per_cell, length = self.flux.shape
        for copy in self.form_copies:
            copy.wait()
        rows = []
        for r, c in self.cells:
            rows += [self.ranges[r, c].astype(jnp.float32), self.widths[r, c : c + 1]]
        filler = -3 * count % 8
        if filler:
            rows.append(jnp.zeros((filler, per_cell), jnp.float32))
        columns = jnp.concatenate(rows, axis=0).T
        step = 16
        position = lax.broadcasted_iota(jnp.int32, (step, length), 1).astype(jnp.float32)
        self.width = []
        for i in range(count):
            low, high, width = (columns[:, 3 * i + j : 3 * i + j + 1] for j in range(3))
            self.width.append(width)
            self.flux_copies[i].wait()
            for row in range(0, per_cell, step):
                inside = (position >= low[row : row + step]) & (position < high[row : row + step])
                kept = jnp.where(inside, self.flux[i, row : row + step].astype(jnp.float32), 0.0)
                start = i * per_cell + row
                self.masked[start : start + step] = kept.astype(jnp.bfloat16)

    def half(self, index, stores):
        _, per_cell, length = self.flux.shape
        per_bin = length // 2 // NKB
        lane = lax.broadcasted_iota(jnp.int32, (1, NKB), 1) * per_bin
        waves = [
            (lane + q).astype(jnp.float32) * (2.0 * jnp.pi / length)
            for q in (2 * index, 2 * index + 1)
        ]
        table = self.table[index]
        tiles = [table[:, i * NKB : (i + 1) * NKB] for i in range(4)]
        later = jnp.concatenate([tiles[0], -tiles[1], tiles[2], -tiles[3]], axis=1)
        raw = jnp.dot(
            self.masked[...],
            jnp.concatenate([table, later], axis=0),
            preferred_element_type=jnp.float32,
        )
        for i in range(len(self.cells)):
            windows = [jnp.exp(-0.5 * (wave * self.width[i]) ** 2) for wave in waves]
            for tile in range(4):
                part = raw[i * per_cell : (i + 1) * per_cell, tile * NKB : (tile + 1) * NKB]
                value = (part * windows[tile % 2]).astype(jnp.bfloat16)
                start = (4 * index + tile) * NKB
                for ref, row in stores[i]:
                    ref[row : row + per_cell, start : start + NKB] = value


def spectra_scratch(count, per_cell, basis, ranges, widths):
    halves, _, _ = basis.shape
    length = 2 * basis.shape[1]
    return [
        pltpu.VMEM((count, per_cell, length), jnp.bfloat16),
        pltpu.VMEM(basis.shape, jnp.bfloat16),
        pltpu.VMEM((count * per_cell, length), jnp.bfloat16),
        pltpu.VMEM(ranges.shape, jnp.int32),
        pltpu.VMEM(widths.shape, jnp.float32),
        pltpu.SemaphoreType.DMA((count,)),
        pltpu.SemaphoreType.DMA((2 + halves,)),
    ]


def vmem(n):
    return [pl.BlockSpec(memory_space=pltpu.VMEM)] * n


def in_hbm(value):
    return pltpu.with_memory_space_constraint(value, pltpu.HBM)


def params():
    return pltpu.CompilerParams(vmem_limit_bytes=VMEM_LIMIT)


def cost(flops, nbytes):
    return pl.CostEstimate(flops=int(flops), bytes_accessed=int(nbytes), transcendentals=0)


def end_cells(forests, ranges, widths, basis):
    _, cols, per_cell, length = forests.shape
    cells = [(0, 0), (0, cols - 1)]

    def kernel(forests, ranges, widths, basis, ends, *scratch):
        spectra = Spectra(cells, forests, basis, ranges, widths, scratch)
        spectra.start()
        spectra.mask()
        for copy in spectra.table_copies:
            copy.wait()
        for index in range(basis.shape[0]):
            spectra.half(index, [[(ends, 0)], [(ends, per_cell)]])

    return pl.pallas_call(
        kernel,
        name="end_cells",
        out_shape=jax.ShapeDtypeStruct((2 * per_cell, length), jnp.bfloat16),
        in_specs=[pl.BlockSpec(memory_space=pltpu.HBM)] * 4,
        out_specs=pl.BlockSpec(memory_space=pltpu.VMEM),
        scratch_shapes=spectra_scratch(2, per_cell, basis, ranges, widths),
        compiler_params=params(),
        cost_estimate=cost(4 * per_cell * length * length, 4 * 2**20),
    )(in_hbm(forests), in_hbm(ranges), in_hbm(widths), in_hbm(basis))


def other_cells(forests, ranges, widths, basis, ends, entries, bins, stages, handed):
    rows, cols, per_cell, length = forests.shape
    slots = bins.shape[0]
    cells = [(0, c) for c in range(1, cols - 1)]
    cells += [(r, c) for r in range(1, rows) for c in range(cols)]
    sizes = [sum(len(group[1]) for group in stage) for stage in stages]
    strip = per_cell * per_cell // length
    n_basis = basis.shape[0]

    def kernel(*refs):
        forests, ranges, widths, basis, ends, entries, bins = refs[:7]
        middle, own, low, counts = refs[7:11]
        sorted_bins, scratch = refs[11 : 11 + len(stages)], refs[11 + len(stages) :]
        entries_here, slot_of, list_sem = scratch[-3:]
        list_copy = pltpu.make_async_copy(entries, entries_here, list_sem)
        list_copy.start()
        spectra = Spectra(cells, forests, basis, ranges, widths, scratch[:-3])
        spectra.start()
        list_copy.wait()

        @pl.loop(0, slots)
        def _(s):
            cell, up, side, live = (entries_here[0, i, 0, s] for i in range(4))
            slot_of[cell * len(OFFSETS) + 3 * up + side] = jnp.where(live > 0, s, s + slots)

        def bins_of(key):
            at = slot_of[key]
            dead = at >= slots
            block = bins[jnp.where(dead, at - slots, at)].astype(jnp.float32)
            return block + jnp.where(dead, float(NSEP), 0.0)

        spectra.mask()
        low[:per_cell] = ends[:per_cell]
        stores = []
        for r, c in cells:
            if r == 0:
                stores.append([(middle, (c - 1) * per_cell)])
                continue
            stores.append([(own, ((r - 1) * cols + c) * per_cell)])
            if c == 0:
                stores[-1].append((low, r * per_cell))
        for copy in spectra.table_copies:
            copy.wait()
        for index in range(n_basis):
            spectra.half(index, stores)
        for target, stage in zip(sorted_bins, stages):
            for i, (center, edge) in enumerate((c, edge) for c, pair in stage for edge in pair):
                block = bins_of(edge[0])
                target[i] = (block if center == edge[1] else block.T).astype(jnp.bfloat16)
        found = [jnp.zeros((8, per_cell), jnp.float32) for _ in range(NSEP)]
        for r, key in enumerate(handed):
            block = bins_of(key)
            for t in range(NSEP):
                one = jnp.where(block == float(t), 1.0, 0.0)
                found[t] = found[t] + one.reshape(per_cell // 8, 8, per_cell).sum(axis=0)
            block = block.astype(jnp.bfloat16)
            start = rows * per_cell + r * strip
            for i in range(per_cell // strip):
                low[start : start + strip, i * per_cell : (i + 1) * per_cell] = (
                    block[i * strip : (i + 1) * strip]
                )
        for t in range(NSEP):
            counts[t] = found[t]

    hbm, anywhere = (pl.BlockSpec(memory_space=space) for space in (pltpu.HBM, pl.ANY))
    bf16, f32 = jnp.bfloat16, jnp.float32
    shapes = [((cols - 2) * per_cell, length), ((rows - 1) * cols * per_cell, length)]
    shapes.append((rows * (per_cell + strip), length))
    shapes = [jax.ShapeDtypeStruct(shape, bf16) for shape in shapes]
    shapes.append(jax.ShapeDtypeStruct((NSEP, 8, per_cell), f32))
    shapes += [jax.ShapeDtypeStruct((size, per_cell, per_cell), bf16) for size in sizes]
    return pl.pallas_call(
        kernel,
        name="other_cells",
        out_shape=shapes,
        in_specs=[hbm] * 4 + vmem(1) + [anywhere] + vmem(1),
        out_specs=vmem(len(shapes)),
        scratch_shapes=spectra_scratch(len(cells), per_cell, basis, ranges, widths)
        + [
            pltpu.SMEM(entries.shape, jnp.int32),
            pltpu.SMEM((slots,), jnp.int32),
            pltpu.SemaphoreType.DMA,
        ],
        compiler_params=params(),
        cost_estimate=cost(2 * len(cells) * per_cell * length * length, 8 * 2**20),
    )(
        in_hbm(forests),
        in_hbm(ranges),
        in_hbm(widths),
        in_hbm(basis),
        ends,
        entries,
        bins,
    )


def pair_sums(groups, given, bins, arrays, place, carried, per_cell, last):
    length = arrays[0].shape[1]
    n_arrays, n_carried = len(arrays), len(carried)
    span = 2 * NKB
    strip = per_cell * per_cell // length

    def kernel(*refs):
        arrays, bins = refs[:n_arrays], refs[n_arrays]
        carried = refs[n_arrays + 1 : n_arrays + 1 + n_carried]
        outs, chosen = refs[n_arrays + 1 + n_carried : -1], refs[-1]
        lane = lax.broadcasted_iota(jnp.int32, (per_cell, NKB), 1)
        unit = jnp.where(lane == 0, 1.0, 0.0).astype(jnp.bfloat16)
        first = lax.broadcasted_iota(jnp.int32, (NSEP, 8, NKB), 2) == 0

        def columns(cell, n):
            array, row = place[cell]
            value = arrays[array][row : row + per_cell, n * span : (n + 1) * span]
            if n != SINE_TILE // 2:
                return value
            return jnp.concatenate([value[:, :NKB] + unit, value[:, NKB:]], axis=1)

        def choose(e, block, row, column):
            for t in range(NSEP):
                start = t * per_cell + row
                e[start : start + block.shape[0], column : column + per_cell] = jnp.where(
                    block == jnp.bfloat16(t), jnp.bfloat16(1), jnp.bfloat16(0)
                )

        def add(sums, e, center, others):
            onehot = e[:, : len(others) * per_cell]
            for n in range(length // span):
                right = jnp.concatenate([columns(other, n) for other in others], axis=0)
                mixed = jnp.dot(onehot, right, preferred_element_type=jnp.float32)
                left = columns(center, n).astype(jnp.float32)
                term = mixed.reshape(NSEP, per_cell, span) * left[None]
                term = term.reshape(NSEP, per_cell // 8, 8, span).sum(axis=1)
                for s in (0, 1):
                    which = int(2 * n + s == SINE_TILE)
                    sums[which] = sums[which] + term[:, :, s * NKB : (s + 1) * NKB]

        def zeros():
            return [jnp.zeros((NSEP, 8, NKB), jnp.float32) for _ in range(2)]

        sums, others_sums = zeros(), zeros()
        position = turn = 0
        for center, pair in groups:
            e = chosen.at[turn % 2]
            turn += 1
            for o in range(len(pair)):
                choose(e, bins[position + o], 0, o * per_cell)
            position += len(pair)
            add(sums, e, center, [edge[1] if center != edge[1] else edge[2] for edge in pair])
        for array, start, a, b in given:
            e = chosen.at[turn % 2]
            turn += 1
            for i in range(per_cell // strip):
                piece = arrays[array][start : start + strip, i * per_cell : (i + 1) * per_cell]
                choose(e, piece, i * strip, 0)
            add(others_sums, e, a, [b])
        if not last:
            for which in (0, 1):
                outs[0][which] = sums[which]
            if given:
                outs[1][...] = binned(others_sums, first)
            return
        *partials, left_out, for_others = carried
        for partial in partials:
            sums = [sums[which] + partial[which] for which in (0, 1)]
        own = binned(sums, first)
        outs[0][...] = own
        outs[1][:NSEP] = own + for_others[...]
        counts = (jnp.where(first, sums[1], 0.0) + left_out[...]).sum(axis=1)
        outs[1][NSEP:] = jnp.broadcast_to(counts.sum(axis=1, keepdims=True), (NSEP, NKB))

    if last:
        shapes = [(NSEP, NKB), (2 * NSEP, NKB)]
    else:
        shapes = [(2, NSEP, 8, NKB)] + [(NSEP, NKB)] * bool(given)
    n_edges = sum(len(group[1]) for group in groups) + len(given)
    return pl.pallas_call(
        kernel,
        out_shape=[jax.ShapeDtypeStruct(shape, jnp.float32) for shape in shapes],
        in_specs=vmem(n_arrays + 1 + n_carried),
        out_specs=vmem(len(shapes)),
        scratch_shapes=[pltpu.VMEM((2, NSEP * per_cell, 2 * per_cell), jnp.bfloat16)],
        compiler_params=params(),
        cost_estimate=cost(2 * NSEP * per_cell * per_cell * length * n_edges, 2**20),
    )(*arrays, bins, *carried)


def over_mesh(value, extra):
    n_ra, n_dec = lax.axis_size("ra"), lax.axis_size("dec")
    if n_dec < 4 or n_dec & (n_dec - 1) or n_ra & (n_ra - 1):
        return lax.psum(value, ("ra", "dec")), shifted(extra, "dec", -1)
    along_ra = [("ra", 1 << k) for k in range(n_ra.bit_length() - 1)]
    along_dec = [("dec", 1 << k) for k in range(1, n_dec.bit_length() - 1)]
    size, here = value.shape[0], lax.axis_index("dec")
    passed = from_left = extra
    for axis, step in [*along_ra[:1], ("dec", 1), *along_dec, *along_ra[1:]]:
        mask = 3 if (axis, step) == ("dec", 2) else step
        message = value
        if axis == "dec":
            message = jnp.concatenate([value, extra if step == 1 else passed], axis=0)
        count = lax.axis_size(axis)
        other = lax.ppermute(message, axis, [(i, i ^ mask) for i in range(count)])
        value = value + other[:size]
        if axis == "dec":
            from_left = jnp.where(here % (2 * step) == step, other[size:], from_left)
            passed = passed if step == 1 else other[size:]
    return value, jnp.where(here == 0, jnp.zeros_like(from_left), from_left)


def shifted(value, axis, steps):
    count = lax.axis_size(axis)
    return lax.ppermute(
        value, axis, [(i + steps, i) for i in range(count) if 0 <= i + steps < count]
    )


def per_device(forests, resolution, pixel_range, block_pairs, block_count, separation_bin):
    rows, cols, per_cell, length = forests.shape
    stages, handed = plan(rows, cols)
    table = dft_table(length, NKB)
    basis = jnp.asarray(table)
    slot = lax.broadcasted_iota(jnp.int32, (1, 1, 1, block_pairs.shape[2]), 3)
    live = (slot < block_count[..., None, None]).astype(jnp.int32)
    entries = jnp.concatenate([block_pairs.transpose(0, 3, 1, 2), live], axis=1)
    ends = end_cells(forests, pixel_range, resolution, basis)
    above_ends = shifted(ends, "ra", 1)
    middle, own, low, counts, *bins = other_cells(
        forests,
        pixel_range,
        resolution,
        basis,
        ends,
        entries,
        separation_bin[0, 0],
        stages,
        handed,
    )
    above_middle = shifted(middle, "ra", 1)
    right = shifted(low, "dec", 1)

    place = {(0, 0): (0, 0), (0, cols - 1): (0, 1)}
    place |= {(0, c): (1, c - 1) for c in range(1, cols - 1)}
    place |= {(r, c): (2, (r - 1) * cols + c) for r in range(1, rows) for c in range(cols)}
    place |= {(r, cols): (3, r) for r in range(rows)}
    place |= {(rows, 0): (4, 0), (rows, cols - 1): (4, 1)}
    place |= {(rows, c): (5, c - 1) for c in range(1, cols - 1)}
    place |= {(rows, cols): (6, 0)}
    strip = per_cell * per_cell // length
    given = [(3, rows * per_cell + r * strip, (r, cols), (r + 1, cols - 1)) for r in range(rows)]

    def sums(stage, arrays, given, carried):
        cells = {cell for _, pair in stages[stage] for edge in pair for cell in edge[1:3]}
        cells |= {cell for one in given for cell in one[2:]}
        named = sorted({place[cell][0] for cell in cells})
        local = {cell: (named.index(place[cell][0]), place[cell][1] * per_cell) for cell in cells}
        return pair_sums(
            stages[stage],
            [(named.index(one[0]), *one[1:]) for one in given],
            bins[stage],
            [arrays[i] for i in named],
            local,
            carried,
            per_cell,
            stage == len(stages) - 1,
        )

    arrays = [ends, middle, own, right, above_ends, above_middle]
    (partial,) = sums(0, arrays, [], [])
    above_ends, partial = lax.optimization_barrier((above_ends, partial))
    arrays[4] = above_ends
    arrays.append(shifted(above_ends[:per_cell], "dec", 1))
    partial_too, for_others = sums(1, arrays, given, [])
    own_sums, result = sums(2, arrays, [], [partial, partial_too, counts, for_others])
    total, from_left = over_mesh(result, for_others)
    tile_power = ((own_sums + from_left) / (per_cell * length)).reshape(1, 1, NSEP, NKB)
    sky_power = total[:NSEP] / jnp.maximum(total[NSEP:], 1.0)
    return tile_power, sky_power


def solution(mesh):
    in_specs = (
        P("ra", "dec", None, None),
        P("ra", "dec", None),
        P("ra", "dec", None, None),
        P("ra", "dec", None, None),
        P("ra", "dec"),
        P("ra", "dec", None, None, None),
    )
    out_specs = (P("ra", "dec", None, None), P())
    return jax.shard_map(
        per_device, mesh=mesh, in_specs=in_specs, out_specs=out_specs, check_vma=False
    )
```

```python
import jax
import jax.numpy as jnp
import numpy as np
from jax import lax
from jax.experimental import pallas as pl
from jax.experimental.pallas import tpu as pltpu
from jax.sharding import PartitionSpec as P

NSEP = 8
NKB = 128
VMEM_LIMIT = 32 * 2**20
OFFSETS = ((0, 0), (0, 1), (1, -1), (1, 0), (1, 1))

SINE_TILE = 2


def dft_table(length, n_bins):
    per_bin = length // 2 // n_bins
    sample = np.arange(length // 2)[:, None]
    blocks = []
    for q in range(0, per_bin, 2):
        modes = [np.arange(n_bins)[None, :] * per_bin + q + s for s in (0, 1)]
        angles = [2.0 * np.pi * (sample * mode % length) / length for mode in modes]
        tiles = [np.cos(angle) for angle in angles] + [np.sin(angle) for angle in angles]
        blocks.append(np.concatenate(tiles, axis=1))
    return np.stack(blocks).astype(np.float32).astype(jnp.bfloat16)


def pair_up(edges):
    at = {}
    for edge in edges:
        for cell in {edge[1], edge[2]}:
            at.setdefault(cell, []).append(edge)
    seen, used, groups, rest = set(), set(), [], []

    def visit(cell, up):
        seen.add(cell)
        pending = []
        for edge in at[cell]:
            if edge in used or edge is up:
                continue
            other = edge[2] if edge[1] == cell else edge[1]
            used.add(edge)
            if other == cell or other in seen or not visit(other, edge):
                pending.append(edge)
        pending.sort(key=lambda edge: edge[3])
        taken = len(pending) % 2 == 1 and up is not None
        if taken:
            pending.append(up)
        elif len(pending) % 2:
            rest.append(pending.pop())
        for i in range(0, len(pending), 2):
            groups.append((cell, pending[i : i + 2]))
        return taken

    for cell in sorted(at, reverse=True):
        if cell not in seen:
            visit(cell, None)
    return groups, rest


def plan(rows, cols):
    def arrival(cell):
        r, c = cell
        if r == rows:
            return 1 if c in (0, cols - 1) else 2
        return 0 if c < cols else 1

    edges, handed = [], []
    for r in range(rows):
        for c in range(cols):
            for d, (up, side) in enumerate(OFFSETS):
                a, b = (r, c), (r + up, c + side)
                key = (r * cols + c) * len(OFFSETS) + d
                if b[1] < 0:
                    handed.append(key)
                else:
                    edges.append((key, a, b, max(arrival(a), arrival(b))))
    stages = [[], [], []]
    groups, rest = pair_up([edge for edge in edges if edge[3] < 2])
    for group in groups:
        stages[max(edge[3] for edge in group[1])].append(group)
    groups, rest = pair_up(rest + [edge for edge in edges if edge[3] == 2])
    stages[2] = groups + [(edge[1], [edge]) for edge in rest]
    return stages, handed


def binned(sums, first):
    return (sums[0] + jnp.where(first, 0.0, sums[1])).sum(axis=1)


class Spectra:
    def __init__(self, cells, forests, basis, ranges, widths, scratch):
        (self.flux, self.table, self.masked, self.ranges, self.widths, sems, more_sems) = scratch
        self.cells = cells
        self.flux_copies = [
            pltpu.make_async_copy(forests.at[r, c], self.flux.at[i], sems.at[i])
            for i, (r, c) in enumerate(cells)
        ]
        self.form_copies = [
            pltpu.make_async_copy(ranges, self.ranges, more_sems.at[0]),
            pltpu.make_async_copy(widths, self.widths, more_sems.at[1]),
        ]
        self.table_copies = [
            pltpu.make_async_copy(basis.at[i], self.table.at[i], more_sems.at[2 + i])
            for i in range(basis.shape[0])
        ]

    def start(self):
        for copy in self.form_copies + self.flux_copies + self.table_copies:
            copy.start()

    def mask(self):
        count, per_cell, length = self.flux.shape
        for copy in self.form_copies:
            copy.wait()
        rows = []
        for r, c in self.cells:
            rows += [self.ranges[r, c].astype(jnp.float32), self.widths[r, c : c + 1]]
        filler = -3 * count % 8
        if filler:
            rows.append(jnp.zeros((filler, per_cell), jnp.float32))
        columns = jnp.concatenate(rows, axis=0).T
        step = 16
        position = lax.broadcasted_iota(jnp.int32, (step, length), 1).astype(jnp.float32)
        self.width = []
        for i in range(count):
            low, high, width = (columns[:, 3 * i + j : 3 * i + j + 1] for j in range(3))
            self.width.append(width)
            self.flux_copies[i].wait()
            for row in range(0, per_cell, step):
                inside = (position >= low[row : row + step]) & (position < high[row : row + step])
                kept = jnp.where(inside, self.flux[i, row : row + step].astype(jnp.float32), 0.0)
                start = i * per_cell + row
                self.masked[start : start + step] = kept.astype(jnp.bfloat16)

    def half(self, index, stores):
        _, per_cell, length = self.flux.shape
        per_bin = length // 2 // NKB
        lane = lax.broadcasted_iota(jnp.int32, (1, NKB), 1) * per_bin
        waves = [
            (lane + q).astype(jnp.float32) * (2.0 * jnp.pi / length)
            for q in (2 * index, 2 * index + 1)
        ]
        table = self.table[index]
        tiles = [table[:, i * NKB : (i + 1) * NKB] for i in range(4)]
        later = jnp.concatenate([tiles[0], -tiles[1], tiles[2], -tiles[3]], axis=1)
        raw = jnp.dot(
            self.masked[...],
            jnp.concatenate([table, later], axis=0),
            preferred_element_type=jnp.float32,
        )
        for i in range(len(self.cells)):
            windows = [jnp.exp(-0.5 * (wave * self.width[i]) ** 2) for wave in waves]
            for tile in range(4):
                part = raw[i * per_cell : (i + 1) * per_cell, tile * NKB : (tile + 1) * NKB]
                value = (part * windows[tile % 2]).astype(jnp.bfloat16)
                start = (4 * index + tile) * NKB
                for ref, row in stores[i]:
                    ref[row : row + per_cell, start : start + NKB] = value


def spectra_scratch(count, per_cell, basis, ranges, widths):
    halves, _, _ = basis.shape
    length = 2 * basis.shape[1]
    return [
        pltpu.VMEM((count, per_cell, length), jnp.bfloat16),
        pltpu.VMEM(basis.shape, jnp.bfloat16),
        pltpu.VMEM((count * per_cell, length), jnp.bfloat16),
        pltpu.VMEM(ranges.shape, jnp.int32),
        pltpu.VMEM(widths.shape, jnp.float32),
        pltpu.SemaphoreType.DMA((count,)),
        pltpu.SemaphoreType.DMA((2 + halves,)),
    ]


def vmem(n):
    return [pl.BlockSpec(memory_space=pltpu.VMEM)] * n


def in_hbm(value):
    return pltpu.with_memory_space_constraint(value, pltpu.HBM)


def params():
    return pltpu.CompilerParams(vmem_limit_bytes=VMEM_LIMIT)


def cost(flops, nbytes):
    return pl.CostEstimate(flops=int(flops), bytes_accessed=int(nbytes), transcendentals=0)


def end_cells(forests, ranges, widths, basis):
    _, cols, per_cell, length = forests.shape
    cells = [(0, 0), (0, cols - 1)]

    def kernel(forests, ranges, widths, basis, ends, *scratch):
        spectra = Spectra(cells, forests, basis, ranges, widths, scratch)
        spectra.start()
        spectra.mask()
        for copy in spectra.table_copies:
            copy.wait()
        for index in range(basis.shape[0]):
            spectra.half(index, [[(ends, 0)], [(ends, per_cell)]])

    return pl.pallas_call(
        kernel,
        name="end_cells",
        out_shape=jax.ShapeDtypeStruct((2 * per_cell, length), jnp.bfloat16),
        in_specs=[pl.BlockSpec(memory_space=pltpu.HBM)] * 4,
        out_specs=pl.BlockSpec(memory_space=pltpu.VMEM),
        scratch_shapes=spectra_scratch(2, per_cell, basis, ranges, widths),
        compiler_params=params(),
        cost_estimate=cost(4 * per_cell * length * length, 4 * 2**20),
    )(in_hbm(forests), in_hbm(ranges), in_hbm(widths), in_hbm(basis))


def other_cells(forests, ranges, widths, basis, ends, entries, bins, stages, handed):
    rows, cols, per_cell, length = forests.shape
    slots = bins.shape[0]
    cells = [(0, c) for c in range(1, cols - 1)]
    cells += [(r, c) for r in range(1, rows) for c in range(cols)]
    sizes = [sum(len(group[1]) for group in stage) for stage in stages]
    strip = per_cell * per_cell // length
    n_basis = basis.shape[0]

    def kernel(*refs):
        forests, ranges, widths, basis, ends, entries, bins = refs[:7]
        middle, own, low, counts = refs[7:11]
        sorted_bins, scratch = refs[11 : 11 + len(stages)], refs[11 + len(stages) :]
        entries_here, slot_of, list_sem = scratch[-3:]
        list_copy = pltpu.make_async_copy(entries, entries_here, list_sem)
        list_copy.start()
        spectra = Spectra(cells, forests, basis, ranges, widths, scratch[:-3])
        spectra.start()
        list_copy.wait()

        @pl.loop(0, slots)
        def _(s):
            cell, up, side, live = (entries_here[0, i, 0, s] for i in range(4))
            slot_of[cell * len(OFFSETS) + 3 * up + side] = jnp.where(live > 0, s, s + slots)

        def bins_of(key):
            at = slot_of[key]
            dead = at >= slots
            block = bins[jnp.where(dead, at - slots, at)].astype(jnp.float32)
            return block + jnp.where(dead, float(NSEP), 0.0)

        spectra.mask()
        low[:per_cell] = ends[:per_cell]
        stores = []
        for r, c in cells:
            if r == 0:
                stores.append([(middle, (c - 1) * per_cell)])
                continue
            stores.append([(own, ((r - 1) * cols + c) * per_cell)])
            if c == 0:
                stores[-1].append((low, r * per_cell))
        for copy in spectra.table_copies:
            copy.wait()
        for index in range(n_basis):
            spectra.half(index, stores)
        for target, stage in zip(sorted_bins, stages):
            for i, (center, edge) in enumerate((c, edge) for c, pair in stage for edge in pair):
                block = bins_of(edge[0])
                target[i] = (block if center == edge[1] else block.T).astype(jnp.bfloat16)
        found = [jnp.zeros((8, per_cell), jnp.float32) for _ in range(NSEP)]
        for r, key in enumerate(handed):
            block = bins_of(key)
            for t in range(NSEP):
                one = jnp.where(block == float(t), 1.0, 0.0)
                found[t] = found[t] + one.reshape(per_cell // 8, 8, per_cell).sum(axis=0)
            block = block.astype(jnp.bfloat16)
            start = rows * per_cell + r * strip
            for i in range(per_cell // strip):
                low[start : start + strip, i * per_cell : (i + 1) * per_cell] = (
                    block[i * strip : (i + 1) * strip]
                )
        for t in range(NSEP):
            counts[t] = found[t]

    hbm, anywhere = (pl.BlockSpec(memory_space=space) for space in (pltpu.HBM, pl.ANY))
    bf16, f32 = jnp.bfloat16, jnp.float32
    shapes = [((cols - 2) * per_cell, length), ((rows - 1) * cols * per_cell, length)]
    shapes.append((rows * (per_cell + strip), length))
    shapes = [jax.ShapeDtypeStruct(shape, bf16) for shape in shapes]
    shapes.append(jax.ShapeDtypeStruct((NSEP, 8, per_cell), f32))
    shapes += [jax.ShapeDtypeStruct((size, per_cell, per_cell), bf16) for size in sizes]
    return pl.pallas_call(
        kernel,
        name="other_cells",
        out_shape=shapes,
        in_specs=[hbm] * 4 + vmem(1) + [anywhere] + vmem(1),
        out_specs=vmem(len(shapes)),
        scratch_shapes=spectra_scratch(len(cells), per_cell, basis, ranges, widths)
        + [
            pltpu.SMEM(entries.shape, jnp.int32),
            pltpu.SMEM((slots,), jnp.int32),
            pltpu.SemaphoreType.DMA,
        ],
        compiler_params=params(),
        cost_estimate=cost(2 * len(cells) * per_cell * length * length, 8 * 2**20),
    )(
        in_hbm(forests),
        in_hbm(ranges),
        in_hbm(widths),
        in_hbm(basis),
        ends,
        entries,
        bins,
    )


def pair_sums(groups, given, bins, arrays, place, carried, per_cell, last):
    length = arrays[0].shape[1]
    n_arrays, n_carried = len(arrays), len(carried)
    buffers = 4 if len(groups) < 8 else 2
    span = 2 * NKB
    strip = per_cell * per_cell // length

    def kernel(*refs):
        arrays, bins = refs[:n_arrays], refs[n_arrays]
        carried = refs[n_arrays + 1 : n_arrays + 1 + n_carried]
        outs, chosen = refs[n_arrays + 1 + n_carried : -1], refs[-1]
        lane = lax.broadcasted_iota(jnp.int32, (per_cell, NKB), 1)
        unit = jnp.where(lane == 0, 1.0, 0.0).astype(jnp.bfloat16)
        first = lax.broadcasted_iota(jnp.int32, (NSEP, 8, NKB), 2) == 0

        def columns(cell, n):
            array, row = place[cell]
            value = arrays[array][row : row + per_cell, n * span : (n + 1) * span]
            if n != SINE_TILE // 2:
                return value
            return jnp.concatenate([value[:, :NKB] + unit, value[:, NKB:]], axis=1)

        def choose(e, block, row, column):
            for t in range(NSEP):
                start = t * per_cell + row
                e[start : start + block.shape[0], column : column + per_cell] = jnp.where(
                    block == jnp.bfloat16(t), jnp.bfloat16(1), jnp.bfloat16(0)
                )

        def add(sums, e, center, others):
            onehot = e[:, : len(others) * per_cell]
            for n in range(length // span):
                right = jnp.concatenate([columns(other, n) for other in others], axis=0)
                mixed = jnp.dot(onehot, right, preferred_element_type=jnp.float32)
                left = columns(center, n).astype(jnp.float32)
                term = mixed.reshape(NSEP, per_cell, span) * left[None]
                term = term.reshape(NSEP, per_cell // 8, 8, span).sum(axis=1)
                for s in (0, 1):
                    which = int(2 * n + s == SINE_TILE)
                    sums[which] = sums[which] + term[:, :, s * NKB : (s + 1) * NKB]

        def zeros():
            return [jnp.zeros((NSEP, 8, NKB), jnp.float32) for _ in range(2)]

        sums, others_sums = zeros(), zeros()
        position = turn = 0
        for center, pair in groups:
            e = chosen.at[turn % buffers]
            turn += 1
            for o in range(len(pair)):
                choose(e, bins[position + o], 0, o * per_cell)
            position += len(pair)
            add(sums, e, center, [edge[1] if center != edge[1] else edge[2] for edge in pair])
        for array, start, a, b in given:
            e = chosen.at[turn % buffers]
            turn += 1
            for i in range(per_cell // strip):
                piece = arrays[array][start : start + strip, i * per_cell : (i + 1) * per_cell]
                choose(e, piece, i * strip, 0)
            add(others_sums, e, a, [b])
        if not last:
            for which in (0, 1):
                outs[0][which] = sums[which]
            if given:
                outs[1][...] = binned(others_sums, first)
            return
        *partials, left_out, for_others = carried
        for partial in partials:
            sums = [sums[which] + partial[which] for which in (0, 1)]
        own = binned(sums, first)
        outs[0][...] = own
        outs[1][:NSEP] = own + for_others[...]
        counts = (jnp.where(first, sums[1], 0.0) + left_out[...]).sum(axis=1)
        outs[1][NSEP:] = jnp.broadcast_to(counts.sum(axis=1, keepdims=True), (NSEP, NKB))

    if last:
        shapes = [(NSEP, NKB), (2 * NSEP, NKB)]
    else:
        shapes = [(2, NSEP, 8, NKB)] + [(NSEP, NKB)] * bool(given)
    n_edges = sum(len(group[1]) for group in groups) + len(given)
    return pl.pallas_call(
        kernel,
        out_shape=[jax.ShapeDtypeStruct(shape, jnp.float32) for shape in shapes],
        in_specs=vmem(n_arrays + 1 + n_carried),
        out_specs=vmem(len(shapes)),
        scratch_shapes=[pltpu.VMEM((buffers, NSEP * per_cell, 2 * per_cell), jnp.bfloat16)],
        compiler_params=params(),
        cost_estimate=cost(2 * NSEP * per_cell * per_cell * length * n_edges, 2**20),
    )(*arrays, bins, *carried)


def over_mesh(value, extra):
    n_ra, n_dec = lax.axis_size("ra"), lax.axis_size("dec")
    if n_dec < 4 or n_dec & (n_dec - 1) or n_ra & (n_ra - 1):
        return lax.psum(value, ("ra", "dec")), shifted(extra, "dec", -1)
    along_ra = [("ra", 1 << k) for k in range(n_ra.bit_length() - 1)]
    along_dec = [("dec", 1 << k) for k in range(1, n_dec.bit_length() - 1)]
    size, here = value.shape[0], lax.axis_index("dec")
    passed = from_left = extra
    for axis, step in [*along_ra[:1], ("dec", 1), *along_dec, *along_ra[1:]]:
        mask = 3 if (axis, step) == ("dec", 2) else step
        message = value
        if axis == "dec":
            message = jnp.concatenate([value, extra if step == 1 else passed], axis=0)
        count = lax.axis_size(axis)
        other = lax.ppermute(message, axis, [(i, i ^ mask) for i in range(count)])
        value = value + other[:size]
        if axis == "dec":
            from_left = jnp.where(here % (2 * step) == step, other[size:], from_left)
            passed = passed if step == 1 else other[size:]
    return value, jnp.where(here == 0, jnp.zeros_like(from_left), from_left)


def shifted(value, axis, steps):
    count = lax.axis_size(axis)
    return lax.ppermute(
        value, axis, [(i + steps, i) for i in range(count) if 0 <= i + steps < count]
    )


def per_device(forests, resolution, pixel_range, block_pairs, block_count, separation_bin):
    rows, cols, per_cell, length = forests.shape
    stages, handed = plan(rows, cols)
    table = dft_table(length, NKB)
    basis = jnp.asarray(table)
    slot = lax.broadcasted_iota(jnp.int32, (1, 1, 1, block_pairs.shape[2]), 3)
    live = (slot < block_count[..., None, None]).astype(jnp.int32)
    entries = jnp.concatenate([block_pairs.transpose(0, 3, 1, 2), live], axis=1)
    ends = end_cells(forests, pixel_range, resolution, basis)
    above_ends = shifted(ends, "ra", 1)
    middle, own, low, counts, *bins = other_cells(
        forests,
        pixel_range,
        resolution,
        basis,
        ends,
        entries,
        separation_bin[0, 0],
        stages,
        handed,
    )
    above_middle = shifted(middle, "ra", 1)
    right = shifted(low, "dec", 1)

    place = {(0, 0): (0, 0), (0, cols - 1): (0, 1)}
    place |= {(0, c): (1, c - 1) for c in range(1, cols - 1)}
    place |= {(r, c): (2, (r - 1) * cols + c) for r in range(1, rows) for c in range(cols)}
    place |= {(r, cols): (3, r) for r in range(rows)}
    place |= {(rows, 0): (4, 0), (rows, cols - 1): (4, 1)}
    place |= {(rows, c): (5, c - 1) for c in range(1, cols - 1)}
    place |= {(rows, cols): (6, 0)}
    strip = per_cell * per_cell // length
    given = [(3, rows * per_cell + r * strip, (r, cols), (r + 1, cols - 1)) for r in range(rows)]

    def sums(stage, arrays, given, carried):
        cells = {cell for _, pair in stages[stage] for edge in pair for cell in edge[1:3]}
        cells |= {cell for one in given for cell in one[2:]}
        named = sorted({place[cell][0] for cell in cells})
        local = {cell: (named.index(place[cell][0]), place[cell][1] * per_cell) for cell in cells}
        return pair_sums(
            stages[stage],
            [(named.index(one[0]), *one[1:]) for one in given],
            bins[stage],
            [arrays[i] for i in named],
            local,
            carried,
            per_cell,
            stage == len(stages) - 1,
        )

    arrays = [ends, middle, own, right, above_ends, above_middle]
    (partial,) = sums(0, arrays, [], [])
    above_ends, partial = lax.optimization_barrier((above_ends, partial))
    arrays[4] = above_ends
    arrays.append(shifted(above_ends[:per_cell], "dec", 1))
    partial_too, for_others = sums(1, arrays, given, [])
    own_sums, result = sums(2, arrays, [], [partial, partial_too, counts, for_others])
    total, from_left = over_mesh(result, for_others)
    tile_power = ((own_sums + from_left) / (per_cell * length)).reshape(1, 1, NSEP, NKB)
    sky_power = total[:NSEP] / jnp.maximum(total[NSEP:], 1.0)
    return tile_power, sky_power


def solution(mesh):
    in_specs = (
        P("ra", "dec", None, None),
        P("ra", "dec", None),
        P("ra", "dec", None, None),
        P("ra", "dec", None, None),
        P("ra", "dec"),
        P("ra", "dec", None, None, None),
    )
    out_specs = (P("ra", "dec", None, None), P())
    return jax.shard_map(
        per_device, mesh=mesh, in_specs=in_specs, out_specs=out_specs, check_vma=False
    )
```
